512 devices in a mesh: ctx: 8 (over y, z_hi), tp: 64 (over x, z_lo, core).
Axes of the slice: x: 4, y: 4, z: 16 (z_hi: 2, z_lo: 8; z = z_hi * 8 + z_lo), core: 2. Of those that a mesh axis runs over, the one named last changes fastest.
Arguments:
- hidden: bfloat16 [2048, 2048], P(('ctx', 'tp')), may hold values from -6 to 6
- w_in: bfloat16 [2048, 8192], P(None, 'tp'), may hold values from -0.125 to 0.125
- w_bc: bfloat16 [2048, 32], replicated, may hold values from -0.125 to 0.125
- w_dt: bfloat16 [64, 2048], P('tp'), may hold values from -0.125 to 0.125
- dt_bias: float32 [64], P('tp'), may hold values from -5 to -3
- a_log: float32 [64], P('tp'), may hold values from -4.6 to 0
- d_skip: float32 [64], P('tp'), may hold values from 0.5 to 1.5
- conv_w: float32 [4, 4096], P(None, 'tp'), may hold values from -3 to 3
- w_out: bfloat16 [4096, 2048], P('tp'), may hold values from -0.09375 to 0.09375
- d_out: bfloat16 [2048, 2048], P(('ctx', 'tp')), may hold values from -6 to 6
Outputs:
- d_hidden: bfloat16 [2048, 2048], P(('ctx', 'tp'))
- d_w_in: float32 [2048, 8192], P(None, 'tp')
- d_w_out: float32 [4096, 2048], P('tp')
- d_w_bc: float32 [2048, 32], replicated
The draws below stay inside these ranges and needn't reach their ends.
All inputs are finite; a program needn't handle non-finite values.
Results may differ from the reference program's by a relative error of at most 0.017.
Values may be sent and summed in bfloat16 or wider, within the bound.
A program may use at most 64 MiB of HBM per device.

```python
import math
import jax
import jax.numpy as jnp
from jax import lax

D = 2048
HEAD_DIM = 64
STATE = 16
CONV = 4
SEQ_DEV = 256
HEADS = 64
INNER = 4096
LENGTH = 2048


def shard_levels(stream_key, dims, shards, low, high):
    level, own = 1.0, jax.random.fold_in(stream_key, 6)
    for axis_at, shards_of in shards:
        heights = jnp.exp(jax.random.uniform(jax.random.fold_in(own, axis_at), (shards_of,), jnp.float32, low / len(shards), high / len(shards)))
        level = level * jnp.repeat(heights, dims[axis_at] // shards_of).reshape([-1 if axis == axis_at else 1 for axis in range(len(dims))])
    return level


def bell_draw(stream_key, dims, scale, reach, split=(), held_as=jnp.bfloat16):
    result = scale * jax.random.normal(stream_key, dims, jnp.float32)
    if split:
        result = result * shard_levels(stream_key, dims, split, -0.22, 0.18)
    return jnp.clip(result, -reach, reach).astype(held_as)


def setup_inputs(seed: int = 0) -> dict:
    seeds = jax.random.split(jax.random.key(seed), 11)
    hidden = bell_draw(seeds[0], (LENGTH, D), 1.0, 6.0, ((0, 512),))
    w_in = bell_draw(seeds[1], (D, 2 * INNER), D ** -0.5, 0.125, ((1, 64),))
    w_bc = bell_draw(seeds[2], (D, 2 * STATE), D ** -0.5, 0.125)
    w_dt = bell_draw(seeds[3], (HEADS, D), D ** -0.5, 0.125, ((0, 64),))
    dt_bias = jnp.clip(-5.0 + 2.0 * jax.random.uniform(seeds[4], (HEADS,), jnp.float32) ** shard_levels(seeds[4], (HEADS,), ((0, 64),), -0.2, 0.2), -5.0, -3.0)
    a_log = jnp.clip(-4.6 + 4.6 * jax.random.uniform(seeds[5], (HEADS,), jnp.float32) ** shard_levels(seeds[5], (HEADS,), ((0, 64),), -0.2, 0.2), -4.6, 0.0)
    d_skip = jnp.clip(0.5 + 1.0 * jax.random.uniform(seeds[6], (HEADS,), jnp.float32) ** shard_levels(seeds[6], (HEADS,), ((0, 64),), -0.2, 0.2), 0.5, 1.5)
    conv_w = bell_draw(seeds[7], (CONV, INNER), CONV ** -0.5, 3.0, ((1, 64),), jnp.float32)
    w_out = bell_draw(seeds[8], (INNER, D), INNER ** -0.5, 0.09375, ((0, 64),))
    d_out = bell_draw(seeds[9], (LENGTH, D), 1.0, 6.0, ((0, 512),))
    return dict(hidden=hidden, w_in=w_in, w_bc=w_bc, w_dt=w_dt, dt_bias=dt_bias, a_log=a_log, d_skip=d_skip, conv_w=conv_w, w_out=w_out, d_out=d_out)


precise = lax.Precision.HIGHEST

def block_ssd(conv_out, steps_dt, b_rows, c_rows, decay_rate, state_in):
    positions = conv_out.shape[0]
    log_keep = jnp.cumsum(steps_dt * decay_rate)
    causal = lax.broadcasted_iota(jnp.int32, (positions, positions), 0) >= lax.broadcasted_iota(jnp.int32, (positions, positions), 1)
    decays = jnp.exp(jnp.where(causal, log_keep[:, None] - log_keep[None, :], -jnp.inf))
    scores = jnp.einsum('in,jn->ij', c_rows, b_rows, precision=precise) * decays
    weighted = steps_dt[:, None] * conv_out
    outputs = jnp.einsum('ij,jp->ip', scores, weighted, precision=precise)
    outputs = outputs + jnp.exp(log_keep)[:, None] * jnp.einsum('in,pn->ip', c_rows, state_in, precision=precise)
    remains = jnp.exp(log_keep[-1] - log_keep)
    state_out = jnp.exp(log_keep[-1]) * state_in + jnp.einsum('j,jp,jn->pn', remains, weighted, b_rows, precision=precise)
    return (outputs, state_out)

def conv_silu(x_raw, conv_w):
    padded = jnp.pad(x_raw, ((CONV - 1, 0), (0, 0)))
    summed = conv_w[0] * padded[0:LENGTH]
    for shift_k in range(1, CONV):
        summed = summed + conv_w[shift_k] * padded[shift_k:shift_k + LENGTH]
    return jax.nn.silu(summed)

def head_scan(conv_out, steps_dt, b_rows, c_rows, decay_rate):
    blocks = LENGTH // SEQ_DEV

    def advance(state_in, elements):
        outputs, state_out = block_ssd(elements[0], elements[1], elements[2], elements[3], decay_rate, state_in)
        return (state_out, outputs)
    starting = jnp.zeros((HEAD_DIM, STATE), jnp.float32)
    elements = (conv_out.reshape(blocks, SEQ_DEV, HEAD_DIM), steps_dt.reshape(blocks, SEQ_DEV), b_rows.reshape(blocks, SEQ_DEV, STATE), c_rows.reshape(blocks, SEQ_DEV, STATE))
    _, outputs = lax.scan(jax.checkpoint(advance), starting, elements)
    return outputs.reshape(LENGTH, HEAD_DIM)

def strand_gate(x_raw, gate_in, b_c, dt_raw, dt_bias, a_log, d_skip, conv_w):
    conv_out = conv_silu(x_raw, conv_w)
    steps_dt = jax.nn.softplus(dt_raw + dt_bias)
    per_head = conv_out.reshape(LENGTH, HEADS, HEAD_DIM)
    outputs = jax.vmap(head_scan, in_axes=(1, 1, None, None, 0), out_axes=1)(per_head, steps_dt, b_c[:, :STATE], b_c[:, STATE:], -jnp.exp(a_log))
    outputs = outputs.reshape(LENGTH, INNER) + jnp.repeat(d_skip, HEAD_DIM) * conv_out
    return outputs * jax.nn.silu(gate_in)

def reference(hidden, w_in, w_bc, w_dt, dt_bias, a_log, d_skip, conv_w, w_out, d_out):
    d_hidden = jnp.zeros((LENGTH, D), jnp.float32)
    d_w_in = jnp.zeros((D, 2 * INNER), jnp.float32)
    d_w_bc = jnp.zeros((D, 2 * STATE), jnp.float32)
    d_w_out = jnp.zeros((INNER, D), jnp.float32)
    strands = ((hidden, d_out, False), (hidden[::-1, ::-1], d_out[::-1, ::-1], True))
    for strand_in, cotangent, mirrored in strands:
        projected = jnp.dot(strand_in, w_in, preferred_element_type=jnp.float32).astype(jnp.bfloat16)
        per_head = projected.reshape(LENGTH, HEADS, 2, HEAD_DIM).astype(jnp.float32)
        x_raw = per_head[:, :, 0].reshape(LENGTH, INNER)
        gate_in = per_head[:, :, 1].reshape(LENGTH, INNER)
        b_c = jnp.dot(strand_in, w_bc, preferred_element_type=jnp.float32)
        dt_raw = jnp.dot(strand_in, w_dt.T, preferred_element_type=jnp.float32)

        def gate_only(x_part, z_part, bc_part, dt_part):
            return strand_gate(x_part, z_part, bc_part, dt_part, dt_bias, a_log, d_skip, conv_w)
        gated, pullback = jax.vjp(gate_only, x_raw, gate_in, b_c, dt_raw)
        gated_low = gated.astype(jnp.bfloat16)
        grad_gate = jnp.dot(cotangent, w_out.T, preferred_element_type=jnp.float32)
        grad_x, grad_z, grad_b, grad_t = pullback(grad_gate)
        grad_proj = jnp.stack([grad_x.reshape(LENGTH, HEADS, HEAD_DIM), grad_z.reshape(LENGTH, HEADS, HEAD_DIM)], axis=2).reshape(LENGTH, 2 * INNER).astype(jnp.bfloat16)
        grad_b_low = grad_b.astype(jnp.bfloat16)
        grad_t_low = grad_t.astype(jnp.bfloat16)
        grad_in = jnp.dot(grad_proj, w_in.T, preferred_element_type=jnp.float32)
        grad_in = grad_in + jnp.dot(grad_b_low, w_bc.T, preferred_element_type=jnp.float32)
        grad_in = grad_in + jnp.dot(grad_t_low, w_dt, preferred_element_type=jnp.float32)
        if mirrored:
            grad_in = grad_in[::-1, ::-1]
        d_hidden = d_hidden + grad_in
        d_w_in = d_w_in + jnp.dot(strand_in.T, grad_proj, preferred_element_type=jnp.float32)
        d_w_bc = d_w_bc + jnp.dot(strand_in.T, grad_b_low, preferred_element_type=jnp.float32)
        d_w_out = d_w_out + jnp.dot(gated_low.T, cotangent, preferred_element_type=jnp.float32)
    scaling = 1.0 / math.sqrt(LENGTH)
    return (d_hidden.astype(jnp.bfloat16), d_w_in * scaling, d_w_out * scaling, d_w_bc * scaling)
```

```python
import math

import jax
import jax.numpy as jnp
from jax import lax
from jax.experimental import pallas as pl
from jax.experimental.pallas import tpu as pltpu
from jax.sharding import PartitionSpec as P

MESH = pl.DeviceIdType.MESH
BF = jnp.bfloat16
F32 = jnp.float32


def place():
    ctx, tp = lax.axis_index("ctx"), lax.axis_index("tp")
    y, zh = ctx // 2, ctx % 2
    x, zl, core = tp // 16, (tp // 2) % 8, tp % 2
    return x, y, zh * 8 + zl, core


def dev(x, y, z, core):
    return (y * 2 + z // 8, x * 16 + (z % 8) * 2 + core)


def greet(peers):
    barrier = pltpu.get_barrier_semaphore()
    for peer in peers:
        pl.semaphore_signal(barrier, inc=1, device_id=peer, device_id_type=MESH)
    pl.semaphore_wait(barrier, len(peers))


def send(src, dst, ssem, rsem, peer):
    copy = pltpu.make_async_remote_copy(src_ref=src, dst_ref=dst, send_sem=ssem, recv_sem=rsem, device_id=peer, device_id_type=MESH)
    copy.start()
    return copy


def gather_kernel(h_ref, g_ref, own_ref, oth_ref, swap, asm, s_core, r_core, zs, zr, xs, xr, cs, cr, ys, yr):
    x, y, z, core = place()
    half = 1024
    right, left = lax.rem(x + 1, 4), lax.rem(x + 3, 4)
    up, down = lax.rem(z + 1, 16), lax.rem(z + 15, 16)
    north, south = lax.rem(y + 1, 4), lax.rem(y + 3, 4)
    other = dev(x, y, z, 1 - core)
    p_up, p_down = dev(x, y, up, core), dev(x, y, down, core)
    p_right, p_left = dev(right, y, z, core), dev(left, y, z, core)
    p_north, p_south = dev(x, north, z, core), dev(x, south, z, core)
    greet([other, p_up, p_down, p_right, p_left, p_north, p_south])

    def blk(xx, zz):
        return 1 + (zz // 8) * 32 + xx * 8 + zz % 8

    mine = pl.ds(pl.multiple_of(core * half, half), half)
    theirs = pl.ds(pl.multiple_of((1 - core) * half, half), half)
    a = send(h_ref.at[:, theirs], swap.at[0], s_core.at[0], r_core.at[0], other)
    b = send(g_ref.at[:, theirs], swap.at[1], s_core.at[1], r_core.at[1], other)
    own_blk = blk(x, z)
    a.wait()
    b.wait()
    for k, ref in ((0, h_ref), (1, g_ref)):
        local = ref[:, mine].astype(F32)
        remote = swap[k].astype(F32)
        first = jnp.where(core == 0, local, remote)
        second = jnp.where(core == 0, remote, local)
        asm[0:4, :] = first
        asm[4:8, :] = second
        own_ref[k, own_blk] = asm[...].astype(BF)

    pend = []

    def cross(b, slot):
        pend.append(send(own_ref.at[:, b], oth_ref.at[:, b], cs.at[slot], cr.at[slot], other))

    def spread(zz, b, slot):
        pend.append(send(own_ref.at[:, b], own_ref.at[:, b], xs.at[0, slot], xr.at[0, slot], p_right))
        pend.append(send(own_ref.at[:, b], own_ref.at[:, b], xs.at[1, slot], xr.at[1, slot], p_left))
        cross(b, slot)

    def landed(b, sem, peer):
        pltpu.make_async_remote_copy(src_ref=own_ref.at[:, b], dst_ref=own_ref.at[:, b], send_sem=cs.at[0], recv_sem=sem, device_id=peer, device_id_type=MESH).wait_recv()

    def x_arrivals(zz, slot, forward_right):
        bl, br = blk(left, zz), blk(right, zz)
        landed(bl, xr.at[0, slot], p_left)
        if forward_right:
            pend.append(send(own_ref.at[:, bl], own_ref.at[:, bl], xs.at[2, slot], xr.at[2, slot], p_right))
        cross(bl, 16 + slot)
        landed(br, xr.at[1, slot], p_right)
        if not forward_right:
            pend.append(send(own_ref.at[:, br], own_ref.at[:, br], xs.at[2, slot], xr.at[2, slot], p_left))
        cross(br, 32 + slot)

    def far_arrival(zz, slot, forward_right):
        bo = blk(lax.rem(x + 2, 4), zz)
        landed(bo, xr.at[2, slot], p_left if forward_right else p_right)
        cross(bo, 48 + slot)

    pend.append(send(own_ref.at[:, own_blk], own_ref.at[:, own_blk], zs.at[0, 0], zr.at[0, 0], p_up))
    pend.append(send(own_ref.at[:, own_blk], own_ref.at[:, own_blk], zs.at[1, 0], zr.at[1, 0], p_down))
    spread(z, own_blk, 0)
    levels = [[(z, 0)]]
    for s in range(1, 9):
        level = []
        zz = lax.rem(z + 16 - s, 16)
        b = blk(x, zz)
        landed(b, zr.at[0, s - 1], p_down)
        if s < 8:
            pend.append(send(own_ref.at[:, b], own_ref.at[:, b], zs.at[0, s], zr.at[0, s], p_up))
        spread(zz, b, s)
        level.append((zz, s))
        if s < 8:
            zz = lax.rem(z + s, 16)
            b = blk(x, zz)
            landed(b, zr.at[1, s - 1], p_up)
            if s < 7:
                pend.append(send(own_ref.at[:, b], own_ref.at[:, b], zs.at[1, s], zr.at[1, s], p_down))
            spread(zz, b, 8 + s)
            level.append((zz, 8 + s))
        levels.append(level)
        for zz, slot in levels[s - 1]:
            x_arrivals(zz, slot, slot % 2 == 0)
        if s >= 2:
            for zz, slot in levels[s - 2]:
                far_arrival(zz, slot, slot % 2 == 0)
    for zz, slot in levels[8]:
        x_arrivals(zz, slot, slot % 2 == 0)
    for s in (7, 8):
        for zz, slot in levels[s]:
            far_arrival(zz, slot, slot % 2 == 0)
    pend.append(send(own_ref.at[:, 64], own_ref.at[:, 0], ys.at[0], yr.at[0], p_north))
    pend.append(send(own_ref.at[:, 1], own_ref.at[:, 65], ys.at[1], yr.at[1], p_south))
    landed(0, yr.at[0], p_south)
    cross(0, 64)
    landed(65, yr.at[1], p_north)
    cross(65, 65)
    for slot in range(66):
        pltpu.make_async_remote_copy(src_ref=own_ref.at[:, 0], dst_ref=oth_ref.at[:, 0], send_sem=cs.at[0], recv_sem=cr.at[slot], device_id=other, device_id_type=MESH).wait_recv()
    for copy in pend:
        copy.wait_send()


def gather(h, g):
    out = jax.ShapeDtypeStruct((2, 66, 8, 1024), BF)
    D = pltpu.SemaphoreType.DMA
    return pl.pallas_call(
        gather_kernel,
        out_shape=(out, out),
        in_specs=[pl.BlockSpec(memory_space=pltpu.VMEM)] * 2,
        out_specs=[pl.BlockSpec(memory_space=pltpu.VMEM)] * 2,
        scratch_shapes=[
            pltpu.VMEM((2, 4, 1024), BF), pltpu.VMEM((8, 1024), F32),
            D((2,)), D((2,)), D((2, 8)), D((2, 8)), D((3, 16)), D((3, 16)), D((66,)), D((66,)), D((2,)), D((2,)),
        ],
        compiler_params=pltpu.CompilerParams(collective_id=0, has_side_effects=True, vmem_limit_bytes=40 << 20),
        name="gather_rows",
    )(h, g)

BF, F32 = jnp.bfloat16, jnp.float32
ROWS, EXT, D, HALF, CH = 512, 528, 2048, 1024, 256


def mm(a, b, dims):
    return lax.dot_general(a, b, (dims, ((), ())), preferred_element_type=F32)


def nn(a, b):
    return mm(a, b, ((1,), (0,)))


def nt(a, b):
    return mm(a, b, ((1,), (1,)))


def tn(a, b):
    return mm(a, b, ((0,), (0,)))


def iota(shape, dim):
    return lax.broadcasted_iota(jnp.int32, shape, dim)


def flipper():
    return (iota((256, 256), 0) + iota((256, 256), 1) == 255).astype(F32).astype(BF)


def tri(lower):
    a, b = iota((CH, CH), 0), iota((CH, CH), 1)
    return ((a >= b) if lower else (a <= b)).astype(F32).astype(BF)


def split3(v):
    h = v.astype(BF)
    m = (v - h.astype(F32)).astype(BF)
    l = (v - h.astype(F32) - m.astype(F32)).astype(BF)
    return h, m, l


def exact_left(t, v):
    h, m, l = split3(v)
    return (nn(t, l) + nn(t, m)) + nn(t, h)


def exact_right(v, t):
    h, m, l = split3(v)
    return (nn(l, t) + nn(m, t)) + nn(h, t)


def fwd_lanes(shape):
    return iota(shape, 1) < 64


def prepare_kernel(at_ref, par_ref, own_ref, oth_ref, wcat_ref, wout_ref, w7_ref,
                   wf_ref, pre_ref, z_ref, dtr_ref, gg_ref, bc_ref, cum_ref, sums_ref, total_ref, x_scr, wo_scr):
    y, core = at_ref[0], at_ref[1]
    bias, rate = par_ref[0], par_ref[1]
    flip = flipper()
    for q in range(8):
        wf_ref[q * 256:(q + 1) * 256, :] = nn(flip, wcat_ref[(7 - q) * 256:(8 - q) * 256, :]).astype(BF)
        wo_scr[0:64, q * 256:(q + 1) * 256] = wout_ref[:, q * 256:(q + 1) * 256]
        wo_scr[64:128, q * 256:(q + 1) * 256] = nn(wout_ref[:, (7 - q) * 256:(8 - q) * 256], flip).astype(BF)
    mine = pl.ds(pl.multiple_of(core * HALF, HALF), HALF)
    theirs = pl.ds(pl.multiple_of((1 - core) * HALF, HALF), HALF)
    h_own, h_oth = own_ref[0:EXT, :], oth_ref[0:EXT, :]
    pf = nn(h_own, wcat_ref[mine, :]) + nn(h_oth, wcat_ref[theirs, :])
    pr = nn(h_own, wf_ref[mine, :]) + nn(h_oth, wf_ref[theirs, :])
    g_own, g_oth = own_ref[EXT:2 * EXT, :], oth_ref[EXT:2 * EXT, :]
    gg = nt(g_own, wo_scr[:, mine]) + nt(g_oth, wo_scr[:, theirs])
    gg = gg[8:8 + ROWS]
    gg_ref[...] = gg
    first = pltpu.roll(pr[:, 0:128], 64, 1)
    lanes = fwd_lanes((EXT, 128))
    x2 = jnp.where(lanes, pf[:, 0:128], first).astype(BF).astype(F32)
    z2 = jnp.where(lanes, pltpu.roll(pf[:, 0:128], 64, 1), pr[:, 0:128]).astype(BF).astype(F32)
    row = iota((EXT, 128), 0)
    outside = ((row < 8) & (y == 0)) | ((row >= 8 + ROWS) & (y == 3))
    x_scr[...] = jnp.where(outside, 0.0, x2)
    pre = w7_ref[0:1, :] * x_scr[5:5 + ROWS, :]
    for k in range(1, 7):
        pre = pre + w7_ref[k:k + 1, :] * x_scr[5 + k:5 + k + ROWS, :]
    pre_ref[...] = pre
    z2 = z2[8:8 + ROWS]
    z_ref[...] = z2
    bf, br = pf[8:8 + ROWS, 128:256], pr[8:8 + ROWS, 128:256]
    bc_ref[0] = bf.astype(BF)
    bc_ref[1] = br.astype(BF)
    lanes = fwd_lanes((ROWS, 128))
    dtr = jnp.where(lanes, bf[:, 32:33], br[:, 32:33]) + bias
    dtr_ref[...] = dtr
    dt = jnp.maximum(dtr, 0.0) + jnp.log1p(jnp.exp(-jnp.abs(dtr)))
    xc = pre * jax.nn.sigmoid(pre)
    u = dt * xc
    dy = gg * (z2 * jax.nn.sigmoid(z2))
    la = dt * rate
    low, upp = tri(True), tri(False)
    lanes = fwd_lanes((CH, 128))
    lane1, lane16 = fwd_lanes((1, 128)), fwd_lanes((16, 128))
    ends, sts, ads = [], [], []
    for c in range(2):
        rows = slice(c * CH, (c + 1) * CH)
        cum = jnp.where(lanes, exact_left(low, la[rows]), exact_left(upp, la[rows]))
        cum_ref[rows, :] = cum
        end = jnp.where(lane1, cum[CH - 1:CH], cum[0:1])
        ru = (jnp.exp(end - cum) * u[rows]).astype(BF)
        ed = (jnp.exp(cum) * dy[rows]).astype(BF)
        b0, b1 = bf[rows].astype(BF), br[rows].astype(BF)
        st = jnp.where(lane16, tn(b0, ru)[0:16], tn(b1, ru)[0:16])
        ad = jnp.where(lane16, tn(b0, ed)[16:32], tn(b1, ed)[16:32])
        sums_ref[c, 0:16, :] = st
        sums_ref[c, 16:32, :] = ad
        ends.append(end)
        sts.append(st)
        ads.append(ad)
    e0, e1 = jnp.exp(ends[0]), jnp.exp(ends[1])
    total_ref[0:16, :] = jnp.where(lane16, e1 * sts[0] + sts[1], e0 * sts[1] + sts[0])
    total_ref[16:32, :] = jnp.where(lane16, ads[0] + e0 * ads[1], ads[1] + e1 * ads[0])
    total_ref[32:40, :] = jnp.broadcast_to(jnp.exp(ends[0] + ends[1]), (8, 128))


def scan_kernel(at_ref, par_ref, all_ref, pre_ref, z_ref, dtr_ref, gg_ref, bc_ref, cum_ref, sums_ref,
                gated_ref, dpre_ref, dz_ref, tail_ref):
    y = at_ref[0]
    rate, skip = par_ref[1], par_ref[2]
    lane16, lane1 = fwd_lanes((16, 128)), fwd_lanes((1, 128))
    s_f = jnp.zeros((16, 128), F32)
    s_r, e_f, e_r = s_f, s_f, s_f
    for k in range(4):
        st, ad, dk = all_ref[k, 0:16, :], all_ref[k, 16:32, :], all_ref[k, 32:33, :]
        s_f = jnp.where(k < y, dk * s_f + st, s_f)
        e_r = jnp.where(k < y, dk * e_r + ad, e_r)
    for k in (3, 2, 1, 0):
        st, ad, dk = all_ref[k, 0:16, :], all_ref[k, 16:32, :], all_ref[k, 32:33, :]
        s_r = jnp.where(k > y, dk * s_r + st, s_r)
        e_f = jnp.where(k > y, dk * e_f + ad, e_f)
    state, adj = jnp.where(lane16, s_f, s_r), jnp.where(lane16, e_f, e_r)
    ends = []
    for c in range(2):
        cum = cum_ref[c * CH:(c + 1) * CH, :]
        ends.append(jnp.exp(jnp.where(lane1, cum[CH - 1:CH], cum[0:1])))
    st0, st1 = sums_ref[0, 0:16, :], sums_ref[1, 0:16, :]
    ad0, ad1 = sums_ref[0, 16:32, :], sums_ref[1, 16:32, :]
    s_in = [jnp.where(lane16, state, ends[1] * state + st1), jnp.where(lane16, ends[0] * state + st0, state)]
    e_out = [jnp.where(lane16, ad1 + ends[1] * adj, adj), jnp.where(lane16, adj, ad0 + ends[0] * adj)]
    s_out = [ends[0] * s_in[0] + st0, ends[1] * s_in[1] + st1]
    lanes = fwd_lanes((CH, 128))
    low, upp = tri(True), tri(False)
    same = ((iota((128, 128), 0) < 64) == (iota((128, 128), 1) < 64)).astype(F32).astype(BF)
    ii, jj = iota((CH, CH), 0), iota((CH, CH), 1)
    for c in range(2):
        rows = slice(c * CH, (c + 1) * CH)
        pre, z, dtr, gg, cum = (r[rows, :] for r in (pre_ref, z_ref, dtr_ref, gg_ref, cum_ref))
        sg, sz = jax.nn.sigmoid(pre), jax.nn.sigmoid(z)
        xc, gate = pre * sg, z * sz
        dt = jnp.maximum(dtr, 0.0) + jnp.log1p(jnp.exp(-jnp.abs(dtr)))
        u, dy = dt * xc, gg * gate
        ub, dyb = u.astype(BF), dy.astype(BF)
        end = jnp.where(lane1, cum[CH - 1:CH], cum[0:1])
        rem, grow = jnp.exp(end - cum), jnp.exp(cum)
        cum_t = cum.T
        sb, eb = s_in[c].astype(BF), e_out[c].astype(BF)
        zero = jnp.zeros_like(dyb)
        y_s, du_s, tails = [], [], []
        for s in range(2):
            bc = bc_ref[s, rows, :]
            b, cc = bc[:, 0:16], bc[:, 16:32]
            col, line = cum[:, 64 * s:64 * s + 1], cum_t[64 * s:64 * s + 1, :]
            mask = (ii >= jj) if s == 0 else (ii <= jj)
            decay = jnp.exp(jnp.where(mask, col - line, -1e30))
            w = (nt(cc, b) * decay).astype(BF)
            rem_c, grow_c = rem[:, 64 * s:64 * s + 1], grow[:, 64 * s:64 * s + 1]
            y_s.append(nn(w, ub) + grow_c * nn(cc, sb))
            du_s.append(tn(w, dyb) + rem_c * nn(b, eb))
            dym = jnp.where(lanes if s == 0 else ~lanes, dy, 0.0).astype(BF)
            um = jnp.where(lanes if s == 0 else ~lanes, u, 0.0).astype(BF)
            ds = (nt(dym, ub) * decay).astype(BF)
            dc = nn(ds, b) + grow_c * nt(dym, sb)
            db = tn(ds, cc) + rem_c * nt(um, eb)
            tails.append((db, dc))
        y2, du = jnp.where(lanes, y_s[0], y_s[1]), jnp.where(lanes, du_s[0], du_s[1])
        inner = dyb.astype(F32) * y2 - ub.astype(F32) * du
        dl = exact_right(inner, same)
        direct = exact_right(du * xc, same)
        const = jnp.sum(e_out[c] * s_out[c], axis=0, keepdims=True)
        const = exact_right(jnp.broadcast_to(const, (16, 128)), same)[0:1]
        dla = jnp.where(lanes, exact_left(upp, dl), exact_left(low, dl)) + const
        ddt = (rate * dla + direct) * jax.nn.sigmoid(dtr)
        dxc = du * dt + skip * dy
        full = y2 + skip * xc
        gated_ref[rows, :] = full * gate
        dz_ref[rows, :] = gg * full * (sz * (1.0 + z * (1.0 - sz)))
        dpre_ref[rows, :] = dxc * (sg * (1.0 + pre * (1.0 - sg)))
        for s in range(2):
            db, dc = tails[s]
            pad = jnp.zeros((CH, 95), F32)
            tail_ref[s, rows, :] = jnp.concatenate([db, dc, ddt[:, 64 * s:64 * s + 1], pad], axis=1)


def finish_kernel(at_ref, edge_ref, own_ref, oth_ref, wcat_ref, wf_ref, w7_ref, gated_ref, dpre_ref, dz_ref, tail_ref,
                  gin_ref, dw_ref, d_scr, ext_scr, gcat, acc):
    y, core, zh = at_ref[0], at_ref[1], at_ref[2]
    flip = flipper()
    scaling = 1.0 / math.sqrt(D)
    d_scr[8:8 + ROWS, :] = dpre_ref[...]
    d_scr[0:8, :] = jnp.where(y == 0, 0.0, edge_ref[0])
    d_scr[8 + ROWS:EXT, :] = jnp.where(y == 3, 0.0, edge_ref[1])
    dx = w7_ref[6:7, :] * d_scr[5:5 + ROWS, :]
    for k in range(1, 7):
        dx = dx + w7_ref[6 - k:7 - k, :] * d_scr[5 + k:5 + k + ROWS, :]
    dz = dz_ref[...]
    lanes = fwd_lanes((ROWS, 128))
    parts = (jnp.where(lanes, dx, pltpu.roll(dz, 64, 1)), jnp.where(lanes, pltpu.roll(dx, 64, 1), dz))
    ext_scr[0:8, :] = jnp.zeros((8, 640), F32)
    ext_scr[8 + ROWS:EXT, :] = jnp.zeros((8, 640), F32)
    for s in range(2):
        gcat[:, s * 256:s * 256 + 128] = parts[s].astype(BF)
        gcat[:, s * 256 + 128:s * 256 + 256] = tail_ref[s].astype(BF)
        ext_scr[8:8 + ROWS, s * 256:s * 256 + 128] = parts[s]
        ext_scr[8:8 + ROWS, s * 256 + 128:s * 256 + 256] = tail_ref[s]
    ext_scr[8:8 + ROWS, 512:640] = gated_ref[...]
    ext = ext_scr[...].astype(BF)
    mine = pl.ds(pl.multiple_of(core * HALF, HALF), HALF)
    theirs = pl.ds(pl.multiple_of((1 - core) * HALF, HALF), HALF)
    acc[0:512, mine] = tn(ext[:, 0:512], own_ref[0:EXT, :])
    acc[0:512, theirs] = tn(ext[:, 0:512], oth_ref[0:EXT, :])
    acc[512:640, mine] = tn(ext[:, 512:640], own_ref[EXT:2 * EXT, :])
    acc[512:640, theirs] = tn(ext[:, 512:640], oth_ref[EXT:2 * EXT, :])
    for q in range(8):
        cols, back = slice(q * 256, (q + 1) * 256), slice((7 - q) * 256, (8 - q) * 256)
        w = acc[0:160, cols] + nn(acc[256:416, back].astype(BF), flip)
        dw_ref[0:128, cols] = (w[0:128] * scaling).astype(BF)
        wb = (w[128:160] * scaling).astype(BF)
        half, m = q // 4, (q % 4) * 2
        gin_ref[half, m * 32:(m + 1) * 32, HALF:HALF + 128] = wb[:, 0:128]
        gin_ref[half, (m + 1) * 32:(m + 2) * 32, HALF:HALF + 128] = wb[:, 128:256]
        w = acc[512:576, cols] + nn(acc[576:640, back].astype(BF), flip)
        dw_ref[128:192, cols] = (w * scaling).astype(BF)
    local = pl.ds(pl.multiple_of(zh * 256, 256), 256)
    for k in range(2):
        g = nt(gcat[local, 0:256], wcat_ref[k * HALF:(k + 1) * HALF, :]) + nt(gcat[local, 256:512], wf_ref[k * HALF:(k + 1) * HALF, :])
        gin_ref[k, :, 0:HALF] = g.astype(BF)


V = pl.BlockSpec(memory_space=pltpu.VMEM)
S = pl.BlockSpec(memory_space=pltpu.SMEM)


def out(*shape, dtype=F32):
    return jax.ShapeDtypeStruct(shape, dtype)


def params():
    return pltpu.CompilerParams(vmem_limit_bytes=56 << 20)


def prepare(at, par, own, oth, wcat, wout, w7, **kw):
    return pl.pallas_call(
        prepare_kernel,
        out_shape=(out(D, 256, dtype=BF), out(ROWS, 128), out(ROWS, 128), out(ROWS, 128), out(ROWS, 128),
                   out(2, ROWS, 128, dtype=BF), out(ROWS, 128), out(2, 32, 128), out(40, 128)),
        in_specs=[S, S] + [V] * 5, out_specs=[V] * 9,
        scratch_shapes=[pltpu.VMEM((EXT, 128), F32), pltpu.VMEM((128, D), BF)],
        compiler_params=params(), name="prepare", **kw,
    )(at, par, own, oth, wcat, wout, w7)


def scan(at, par, everything, pre, z, dtr, gg, bc, cum, sums, **kw):
    return pl.pallas_call(
        scan_kernel,
        out_shape=(out(ROWS, 128), out(ROWS, 128), out(ROWS, 128), out(2, ROWS, 128)),
        in_specs=[S, S] + [V] * 8, out_specs=[V] * 4,
        compiler_params=params(), name="scan", **kw,
    )(at, par, everything, pre, z, dtr, gg, bc, cum, sums)


def finish(at, edge, own, oth, wcat, wf, w7, gated, dpre, dz, tail, **kw):
    return pl.pallas_call(
        finish_kernel,
        out_shape=(out(2, 256, HALF + 128, dtype=BF), out(192, D, dtype=BF)),
        in_specs=[S] + [V] * 10, out_specs=[V] * 2,
        scratch_shapes=[pltpu.VMEM((EXT, 128), F32), pltpu.VMEM((EXT, 640), F32), pltpu.VMEM((ROWS, 512), BF), pltpu.VMEM((640, D), F32)],
        compiler_params=params(), name="finish", **kw,
    )(at, edge, own, oth, wcat, wf, w7, gated, dpre, dz, tail)


def weights(w_in, w_bc, w_dt, conv_w):
    wcat = jnp.concatenate([w_in, w_bc, w_dt.T, jnp.zeros((D, 95), BF)], axis=1)
    gap = jnp.zeros((3, 64), F32)
    w7 = jnp.concatenate([jnp.concatenate([conv_w, gap], 0), jnp.concatenate([gap, conv_w[::-1]], 0)], axis=1)
    return wcat, jnp.concatenate([w7, jnp.zeros((1, 128), F32)], axis=0)

def ring_y(x, y, z, core):
    return [dev(x, lax.rem(y + k, 4), z, core) for k in (1, 2, 3)]


def states_kernel(total_ref, all_ref, ss, rs):
    x, y, z, core = place()
    peers = ring_y(x, y, z, core)
    greet(peers)
    all_ref[y] = total_ref[...]
    copies = [send(total_ref, all_ref.at[y], ss.at[k], rs.at[k], peers[k]) for k in range(3)]
    for k in range(3):
        copies[k].wait_send()
        came = lax.rem(y + 3 - k, 4)
        pltpu.make_async_remote_copy(src_ref=total_ref, dst_ref=all_ref.at[came], send_sem=ss.at[k], recv_sem=rs.at[k], device_id=peers[k], device_id_type=MESH).wait_recv()


def edges_kernel(dpre_ref, edge_ref, ss, rs):
    x, y, z, core = place()
    north, south = dev(x, lax.rem(y + 1, 4), z, core), dev(x, lax.rem(y + 3, 4), z, core)
    greet([north, south])
    a = send(dpre_ref.at[ROWS - 8:ROWS, :], edge_ref.at[0], ss.at[0], rs.at[0], north)
    b = send(dpre_ref.at[0:8, :], edge_ref.at[1], ss.at[1], rs.at[1], south)
    a.wait()
    b.wait()


def reduce_kernel(gin_ref, dw_ref, hid_ref, dwo_ref, fg_ref,
                  rc, w1, rx, w2, rz, hs, hr, fy, ry, e1, k1, e2,
                  cs, cr, xs, xr, zs, zr, ys, yr, fs, fr, es, er):
    x, y, z, core = place()
    zh, zl = z // 8, z % 8
    other = dev(x, y, z, 1 - core)
    xp = [dev(lax.rem(x + k, 4), y, z, core) for k in (1, 2, 3)]
    yp = ring_y(x, y, z, core)
    zp = [dev(x, y, zh * 8 + lax.rem(zl + k, 8), core) for k in range(1, 8)]
    greet([other] + xp + yp + zp)
    pend = []

    def go(src, dst, ssem, rsem, peer):
        copy = send(src, dst, ssem, rsem, peer)
        pend.append(copy)
        return copy

    near, far = dev(x, y + 1 - 2 * lax.rem(y, 2), z, core), dev(x, 3 - y, z, core)
    turn, side = lax.rem((y + 1) // 2, 2), y // 2
    plan = ((near, turn, far, side), (far, side, near, turn))

    def rows_of(k):
        return pl.ds(pl.multiple_of(k * 96, 96), 96)

    def cols_of(h, k):
        return pl.ds(pl.multiple_of(h * 1024 + k * 512, 512), 512)

    dc = go(gin_ref.at[1 - core], rc, cs.at[0], cr.at[0], other)
    s1 = []
    for h in range(2):
        p1, k1h, _, _ = plan[h]
        s1.append(go(dw_ref.at[rows_of(1 - k1h), h * 1024:(h + 1) * 1024], e1.at[h], es.at[h, 0], er.at[h, 0], p1))
    dc.wait_recv()
    for k in range(4):
        w1[k] = (gin_ref[core, k * 64:(k + 1) * 64, :].astype(F32) + rc[k * 64:(k + 1) * 64, :].astype(F32)).astype(BF)
    sx = [go(w1.at[lax.rem(x + k, 4)], rx.at[k - 1], xs.at[k - 1], xr.at[k - 1], xp[k - 1]) for k in (1, 2, 3)]
    s2 = []
    for h in range(2):
        _, k1h, p2, k2h = plan[h]
        s1[h].wait_recv()
        for q in range(2):
            c = slice(h * 1024 + q * 512, h * 1024 + (q + 1) * 512)
            k1[h, q] = (dw_ref[rows_of(k1h), c].astype(F32) + e1[h, :, q * 512:(q + 1) * 512].astype(F32)).astype(BF)
        s2.append(go(k1.at[h, 1 - k2h], e2.at[h], es.at[h, 1], er.at[h, 1], p2))
    for c in sx:
        c.wait_recv()
    for k in range(8):
        r = slice(k * 8, (k + 1) * 8)
        w2[k] = (w1[x, r, :].astype(F32) + rx[0, r, :].astype(F32) + rx[1, r, :].astype(F32) + rx[2, r, :].astype(F32)).astype(BF)
    sz = [go(w2.at[lax.rem(zl + k, 8)], rz.at[k - 1], zs.at[k - 1], zr.at[k - 1], zp[k - 1]) for k in range(1, 8)]
    s3 = []
    for h in range(2):
        _, k1h, p2, k2h = plan[h]
        s2[h].wait_recv()
        place_q = (rows_of(k1h), cols_of(h, k2h))
        dwo_ref[place_q] = (k1[h, k2h].astype(F32) + e2[h].astype(F32)).astype(BF)
        s3.append(go(dwo_ref.at[place_q], dwo_ref.at[place_q], es.at[h, 2], er.at[h, 2], p2))
    for c in sz:
        c.wait_recv()
    total = w2[zl].astype(F32)
    for k in range(7):
        total = total + rz[k].astype(F32)
    hs[...] = total[:, 0:1024].astype(BF)
    sh = go(hs, hr, cs.at[1], cr.at[1], other)
    fy[...] = total[:, 1024:1152]
    sy = [go(fy, ry.at[k], ys.at[k], yr.at[k], yp[k]) for k in range(3)]

    def arrived(dst, sem, peer):
        pltpu.make_async_remote_copy(src_ref=dst, dst_ref=dst, send_sem=cs.at[0], recv_sem=sem, device_id=peer, device_id_type=MESH).wait_recv()

    s4 = []
    for h in range(2):
        p1, k1h, p2, k2h = plan[h]
        theirs = (rows_of(k1h), cols_of(h, 1 - k2h))
        arrived(dwo_ref.at[theirs], er.at[h, 2], p2)
        block = (rows_of(k1h), slice(h * 1024, (h + 1) * 1024))
        s4.append(go(dwo_ref.at[block], dwo_ref.at[block], es.at[h, 3], er.at[h, 3], p1))
    for c in sy:
        c.wait_recv()
    at = x * 8 + zl
    fg_ref[core, at] = (fy[...] + ry[0] + ry[1] + ry[2]).astype(BF)
    for k in range(1, 8):
        go(fg_ref.at[core, at], fg_ref.at[core, at], fs.at[k - 1], fr.at[k - 1], zp[k - 1])
    sh.wait_recv()
    mine, theirs = hs[...].astype(F32), hr[...].astype(F32)
    mine = jnp.where(core == 0, mine[0:4], mine[4:8])
    theirs = jnp.where(core == 0, theirs[0:4], theirs[4:8])
    hid_ref[:, 0:1024] = jnp.where(core == 0, mine, theirs).astype(BF)
    hid_ref[:, 1024:2048] = jnp.where(core == 0, theirs, mine).astype(BF)
    for k in range(1, 8):
        arrived(fg_ref.at[core, x * 8 + lax.rem(zl + 8 - k, 8)], fr.at[k - 1], zp[k - 1])
    column = pl.ds(x * 8, 8)
    for k in (1, 2, 3):
        go(fg_ref.at[core, column], fg_ref.at[core, column], fs.at[6 + k], fr.at[6 + k], xp[k - 1])
    for k in (1, 2, 3):
        arrived(fg_ref.at[core, pl.ds(lax.rem(x + 4 - k, 4) * 8, 8)], fr.at[6 + k], xp[k - 1])
    go(fg_ref.at[core], fg_ref.at[core], cs.at[2], cr.at[2], other)
    arrived(fg_ref.at[1 - core], cr.at[2], other)
    for h in range(2):
        p1, k1h, _, _ = plan[h]
        arrived(dwo_ref.at[rows_of(1 - k1h), h * 1024:(h + 1) * 1024], er.at[h, 3], p1)
    for copy in pend:
        copy.wait_send()


DMA = pltpu.SemaphoreType.DMA


def remote(cid, mib=32):
    return pltpu.CompilerParams(collective_id=cid, has_side_effects=True, vmem_limit_bytes=mib << 20)


def states(total):
    return pl.pallas_call(
        states_kernel, out_shape=out(4, 40, 128), in_specs=[V], out_specs=V,
        scratch_shapes=[DMA((3,)), DMA((3,))], compiler_params=remote(1), name="states",
    )(total)


def edges(dpre):
    return pl.pallas_call(
        edges_kernel, out_shape=out(2, 8, 128), in_specs=[V], out_specs=V,
        scratch_shapes=[DMA((2,)), DMA((2,))], compiler_params=remote(2), name="edges",
    )(dpre)


def reduce(gin, dw):
    W = HALF + 128
    vm = pltpu.VMEM
    return pl.pallas_call(
        reduce_kernel,
        out_shape=(out(4, D, dtype=BF), out(192, D, dtype=BF), out(2, 32, 8, 128, dtype=BF)),
        in_specs=[V] * 2, out_specs=[V] * 3,
        scratch_shapes=[
            vm((256, W), BF), vm((4, 64, W), BF), vm((3, 64, W), BF), vm((8, 8, W), BF), vm((7, 8, W), BF),
            vm((8, 1024), BF), vm((8, 1024), BF), vm((8, 128), F32), vm((3, 8, 128), F32),
            vm((2, 96, 1024), BF), vm((2, 2, 96, 512), BF), vm((2, 96, 512), BF),
            DMA((3,)), DMA((3,)), DMA((3,)), DMA((3,)), DMA((7,)), DMA((7,)), DMA((3,)), DMA((3,)), DMA((10,)), DMA((10,)), DMA((2, 4)), DMA((2, 4)),
        ],
        compiler_params=remote(3), name="reduce",
    )(gin, dw)


def local(hidden, w_in, w_bc, w_dt, dt_bias, a_log, d_skip, conv_w, w_out, d_out):
    ctx, tp = lax.axis_index("ctx"), lax.axis_index("tp")
    at = jnp.stack([ctx // 2, tp % 2, ctx % 2, 0]).astype(jnp.int32)
    par = jnp.concatenate([dt_bias, -jnp.exp(a_log), d_skip, jnp.zeros((1,), F32)])
    wcat, w7 = weights(w_in, w_bc, w_dt, conv_w)
    own, oth = gather(hidden, d_out)
    own, oth = own.reshape(2 * EXT, HALF), oth.reshape(2 * EXT, HALF)
    wf, pre, z, dtr, gg, bc, cum, sums, total = prepare(at, par, own, oth, wcat, w_out, w7)
    everything = states(total)
    gated, dpre, dz, tail = scan(at, par, everything, pre, z, dtr, gg, bc, cum, sums)
    edge = edges(dpre)
    gin, dw = finish(at, edge, own, oth, wcat, wf, w7, gated, dpre, dz, tail)
    d_hidden, dw, shared = reduce(gin, dw)
    d_w_in = dw[0:128].T.astype(F32)
    d_w_out = dw[128:192].astype(F32)
    d_w_bc = shared.reshape(2, 8, 32, 128).transpose(0, 1, 3, 2).reshape(D, 2 * 16).astype(F32)
    return (d_hidden, d_w_in, d_w_out, d_w_bc)


def solution(mesh):
    in_specs = (
        P(("ctx", "tp"), None), P(None, "tp"), P(), P("tp", None), P("tp"), P("tp"), P("tp"), P(None, "tp"),
        P("tp", None), P(("ctx", "tp"), None),
    )
    out_specs = (P(("ctx", "tp"), None), P(None, "tp"), P("tp", None), P())
    return jax.shard_map(local, mesh=mesh, in_specs=in_specs, out_specs=out_specs, check_vma=False)
```

```python
import math

import jax
import jax.numpy as jnp
from jax import lax
from jax.experimental import pallas as pl
from jax.experimental.pallas import tpu as pltpu
from jax.sharding import PartitionSpec as P

MESH = pl.DeviceIdType.MESH
BF, F32 = jnp.bfloat16, jnp.float32
ROWS, EXT, D, HALF, CH = 512, 528, 2048, 1024, 256
SCALING = 1.0 / math.sqrt(D)


def place():
    ctx, tp = lax.axis_index("ctx"), lax.axis_index("tp")
    y, zh = ctx // 2, ctx % 2
    x, zl, core = tp // 16, (tp // 2) % 8, tp % 2
    return x, y, zh * 8 + zl, core


def dev(x, y, z, core):
    return (y * 2 + z // 8, x * 16 + (z % 8) * 2 + core)


def greet(peers):
    barrier = pltpu.get_barrier_semaphore()
    for peer in peers:
        pl.semaphore_signal(barrier, inc=1, device_id=peer, device_id_type=MESH)
    pl.semaphore_wait(barrier, len(peers))


def remote(src, dst, ssem, rsem, peer):
    return pltpu.make_async_remote_copy(src_ref=src, dst_ref=dst, send_sem=ssem, recv_sem=rsem, device_id=peer, device_id_type=MESH)


def mm(a, b, dims):
    return lax.dot_general(a, b, (dims, ((), ())), preferred_element_type=F32)


def nn(a, b):
    return mm(a, b, ((1,), (0,)))


def nt(a, b):
    return mm(a, b, ((1,), (1,)))


def tn(a, b):
    return mm(a, b, ((0,), (0,)))


def iota(shape, dim):
    return lax.broadcasted_iota(jnp.int32, shape, dim)


def ones_where(mask):
    return mask.astype(F32).astype(BF)


def split3(v):
    h = v.astype(BF)
    m = (v - h.astype(F32)).astype(BF)
    l = (v - h.astype(F32) - m.astype(F32)).astype(BF)
    return h, m, l


def exact_left(t, v):
    h, m, l = split3(v)
    return (nn(t, l) + nn(t, m)) + nn(t, h)


def exact_right(v, t):
    h, m, l = split3(v)
    return (nn(l, t) + nn(m, t)) + nn(h, t)


def fwd_lanes(shape):
    return iota(shape, 1) < 64


def softplus(v):
    return jnp.maximum(v, 0.0) + jnp.log1p(jnp.exp(-jnp.abs(v)))


def sigmoid(v):
    return jax.nn.sigmoid(v)


def mixer_kernel(h_ref, g_ref, win_ref, wbc_ref, wdt_ref, bias_ref, alog_ref, skip_ref, conv_ref, wout_ref,
                 hid_ref, dwi_ref, dwo_ref, fg_ref,
                 swap, asm, own, oth, hown, hoth, wcat, wf, wo, x_scr, d_scr,
                 pre_s, z_s, dtr_s, gg_s, bc_s, cum_s, total_s, all_s, gated_s, dpre_s, dz_s, tail_s, edge_s,
                 gcat, acc, dwi, dwo, gin, rc, w1, rx, w2, rz, hs, hr,
                 fb, fc, f1, fx, f2, fz, fy, ry, ei1, ki1, ei2, eo1, ko1, eo2,
                 sw_s, sw_r, zs, zr, xs, xr, cs, cr, ys, yr, hs_s, hs_r, st_s, st_r, ed_s, ed_r,
                 dc_s, dc_r, dx_s, dx_r, dz_ss, dz_rr, fc_s, fc_r, fx_s, fx_r, fz_s, fz_r, fy_s, fy_r, ga_s, ga_r,
                 ei_s, ei_r, eo_s, eo_r):
    x, y, z, core = place()
    zh, zl = z // 8, z % 8
    bias, rate, skip = bias_ref[...], -jnp.exp(alog_ref[...]), skip_ref[...]
    other = dev(x, y, z, 1 - core)
    xp = [dev(lax.rem(x + k, 4), y, z, core) for k in (1, 2, 3)]
    yp = [dev(x, lax.rem(y + k, 4), z, core) for k in (1, 2, 3)]

    def along(k):
        return dev(x, y, lax.rem(z + 16 + k, 16), core)

    def line(k):
        return dev(x, y, zh * 8 + lax.rem(zl + k, 8), core)

    mine = pl.ds(pl.multiple_of(core * HALF, HALF), HALF)
    theirs = pl.ds(pl.multiple_of((1 - core) * HALF, HALF), HALF)
    pend = []

    def go(src, dst, ssem, rsem, peer):
        copy = remote(src, dst, ssem, rsem, peer)
        copy.start()
        pend.append(copy)
        return copy

    def arrived(dst, rsem):
        remote(dst, dst, sw_s.at[0], rsem, other).wait_recv()

    greet([other] + xp + yp + [along(k) for k in (-3, -2, -1, 1, 2, 3)] + [line(k) for k in range(1, 8)])

    go(h_ref.at[:, theirs], swap.at[0], sw_s.at[0], sw_r.at[0], other)
    go(g_ref.at[:, theirs], swap.at[1], sw_s.at[1], sw_r.at[1], other)

    def blk(xx, k):
        zz = lax.rem(z + 16 + k, 16)
        return (zz // 8) * 32 + xx * 8 + zz % 8

    home = blk(x, 0)
    arrived(swap.at[0], sw_r.at[0])
    arrived(swap.at[1], sw_r.at[1])
    for k, ref in ((0, h_ref), (1, g_ref)):
        here, there = ref[:, mine].astype(F32), swap[k].astype(F32)
        asm[0:4, :] = jnp.where(core == 0, here, there)
        asm[4:8, :] = jnp.where(core == 0, there, here)
        own[k, home] = asm[...].astype(BF)

    def slot(k):
        return k if k >= 0 else 7 - k

    def cross(b, n):
        go(own.at[:, b], oth.at[:, b], cs.at[n], cr.at[n], other)

    def carry(k, far):
        b, n = blk(x, k), slot(k - far)
        go(own.at[:, b], own.at[:, b], zs.at[n], zr.at[n], along(far))

    def spread(k):
        b, n = blk(x, k), slot(k)
        for j in (2, 1, 3):
            go(own.at[:, b], own.at[:, b], xs.at[j - 1, n], xr.at[j - 1, n], xp[j - 1])
        cross(b, n)

    def z_arrival(k):
        arrived(own.at[:, blk(x, k)], zr.at[slot(k)])

    def x_arrivals(k):
        n = slot(k)
        for j in (1, 3, 2):
            b = blk(lax.rem(x + 4 - j, 4), k)
            arrived(own.at[:, b], xr.at[j - 1, n])
            cross(b, 16 * j + n)

    for far in (3, -3, 2, -2, 1, -1):
        carry(0, far)
    spread(0)

    flip = ones_where(iota((256, 256), 0) + iota((256, 256), 1) == 255)
    pick = ones_where(iota((8, 128), 1) == jnp.where(iota((8, 128), 0) == 0, 32, -1))
    for q in range(8):
        r, back = slice(q * 256, (q + 1) * 256), slice((7 - q) * 256, (8 - q) * 256)
        wcat[r, 0:128] = win_ref[r, :]
        steps = tn(jnp.broadcast_to(wdt_ref[:, r].astype(F32), (8, 256)).astype(BF), pick)
        shared = jnp.concatenate([wbc_ref[r, :].astype(F32), jnp.zeros((256, 96), F32)], axis=1)
        wcat[r, 128:256] = (shared + steps).astype(BF)
        wo[0:64, r] = wout_ref[:, r]
        wo[64:128, r] = nn(wout_ref[:, back], flip).astype(BF)
    for q in range(8):
        wf[q * 256:(q + 1) * 256, :] = nn(flip, wcat[(7 - q) * 256:(8 - q) * 256, :]).astype(BF)
    gap = jnp.zeros((1, 64), F32)
    taps = []
    for k in range(7):
        f_tap = conv_ref[k:k + 1, :] if k < 4 else gap
        r_tap = conv_ref[6 - k:7 - k, :] if k >= 3 else gap
        taps.append(jnp.concatenate([f_tap, r_tap], axis=1))

    for k in (-3, 3):
        z_arrival(k)
        step = 1 if k < 0 else -1
        for far in (3, 2, 1):
            carry(k, step * far)
    for k in (-3, 3):
        spread(k)
    for k in (-1, 1, -2, 2):
        z_arrival(k)
        spread(k)
    x_arrivals(0)
    for k in (-6, 6):
        z_arrival(k)
        if k < 0:
            carry(k, 2)
            carry(k, 1)
        else:
            carry(k, -1)
    for k in (-6, 6):
        spread(k)
    for k in (-4, 4, -5, 5):
        z_arrival(k)
        spread(k)
    for k in (-3, 3, -1, 1, -2, 2):
        x_arrivals(k)
    for k in (-7, 7, -8):
        z_arrival(k)
        spread(k)
    for k in (-6, 6, -4, 4, -5, 5, -7, 7, -8):
        x_arrivals(k)
    go(own.at[0, 63], hown.at[0], ys.at[0], yr.at[0], yp[0])
    go(own.at[0, 0], hown.at[1], ys.at[1], yr.at[1], yp[2])
    for n in range(64):
        arrived(oth.at[:, 0], cr.at[n])

    h_own, h_oth = own[0].reshape(ROWS, HALF), oth[0].reshape(ROWS, HALF)
    g_own, g_oth = own[1].reshape(ROWS, HALF), oth[1].reshape(ROWS, HALF)
    gg = nt(g_own, wo[:, mine]) + nt(g_oth, wo[:, theirs])
    gg_s[...] = gg
    for j in range(2):
        arrived(hown.at[j], yr.at[j])
        go(hown.at[j], hoth.at[j], hs_s.at[j], hs_r.at[j], other)
    pf = nn(h_own, wcat[mine, :]) + nn(h_oth, wcat[theirs, :])
    pr = nn(h_own, wf[mine, :]) + nn(h_oth, wf[theirs, :])
    lanes = fwd_lanes((ROWS, 128))
    x2 = jnp.where(lanes, pf[:, 0:128], pltpu.roll(pr[:, 0:128], 64, 1)).astype(BF).astype(F32)
    z2 = jnp.where(lanes, pltpu.roll(pf[:, 0:128], 64, 1), pr[:, 0:128]).astype(BF).astype(F32)
    x_scr[8:8 + ROWS, :] = x2
    z_s[...] = z2
    bf, br = pf[:, 128:256], pr[:, 128:256]
    bc_s[0] = bf.astype(BF)
    bc_s[1] = br.astype(BF)
    dtr = jnp.where(lanes, bf[:, 32:33], br[:, 32:33]) + bias
    dtr_s[...] = dtr
    dt = softplus(dtr)
    la = dt * rate
    dy = gg * (z2 * sigmoid(z2))
    for j in range(2):
        arrived(hoth.at[j], hs_r.at[j])
    e_own, e_oth = hown[...].reshape(16, HALF), hoth[...].reshape(16, HALF)
    xf = nn(e_own, wcat[mine, 0:128]) + nn(e_oth, wcat[theirs, 0:128])
    xb = nn(e_own, wf[mine, 0:128]) + nn(e_oth, wf[theirs, 0:128])
    edge = jnp.where(fwd_lanes((16, 128)), xf, pltpu.roll(xb, 64, 1)).astype(BF).astype(F32)
    x_scr[0:8, :] = jnp.where(y == 0, 0.0, edge[0:8])
    x_scr[8 + ROWS:EXT, :] = jnp.where(y == 3, 0.0, edge[8:16])
    pre = taps[0] * x_scr[5:5 + ROWS, :]
    for k in range(1, 7):
        pre = pre + taps[k] * x_scr[5 + k:5 + k + ROWS, :]
    pre_s[...] = pre
    u = dt * (pre * sigmoid(pre))

    low = ones_where(iota((CH, CH), 0) >= iota((CH, CH), 1))
    upp = ones_where(iota((CH, CH), 0) <= iota((CH, CH), 1))
    lanes, lane1, lane16 = fwd_lanes((CH, 128)), fwd_lanes((1, 128)), fwd_lanes((16, 128))
    ends, sts, ads = [], [], []
    for c in range(2):
        rows = slice(c * CH, (c + 1) * CH)
        cum = jnp.where(lanes, exact_left(low, la[rows]), exact_left(upp, la[rows]))
        cum_s[rows, :] = cum
        end = jnp.where(lane1, cum[CH - 1:CH], cum[0:1])
        ru = (jnp.exp(end - cum) * u[rows]).astype(BF)
        ed = (jnp.exp(cum) * dy[rows]).astype(BF)
        b0, b1 = bf[rows].astype(BF), br[rows].astype(BF)
        sts.append(jnp.where(lane16, tn(b0, ru)[0:16], tn(b1, ru)[0:16]))
        ads.append(jnp.where(lane16, tn(b0, ed)[16:32], tn(b1, ed)[16:32]))
        ends.append(end)
    e0, e1 = jnp.exp(ends[0]), jnp.exp(ends[1])
    total_s[0:16, :] = jnp.where(lane16, e1 * sts[0] + sts[1], e0 * sts[1] + sts[0])
    total_s[16:32, :] = jnp.where(lane16, ads[0] + e0 * ads[1], ads[1] + e1 * ads[0])
    total_s[32:40, :] = jnp.broadcast_to(jnp.exp(ends[0] + ends[1]), (8, 128))
    all_s[y] = total_s[...]
    for k in range(3):
        go(total_s, all_s.at[y], st_s.at[k], st_r.at[k], yp[k])
    for k in range(3):
        arrived(all_s.at[lax.rem(y + 3 - k, 4)], st_r.at[k])
    nil = jnp.zeros((16, 128), F32)
    s_f, s_r, e_f, e_r = nil, nil, nil, nil
    for k in range(4):
        st, ad, dk = all_s[k, 0:16, :], all_s[k, 16:32, :], all_s[k, 32:33, :]
        s_f = jnp.where(k < y, dk * s_f + st, s_f)
        e_r = jnp.where(k < y, dk * e_r + ad, e_r)
    for k in (3, 2, 1, 0):
        st, ad, dk = all_s[k, 0:16, :], all_s[k, 16:32, :], all_s[k, 32:33, :]
        s_r = jnp.where(k > y, dk * s_r + st, s_r)
        e_f = jnp.where(k > y, dk * e_f + ad, e_f)
    state, adj = jnp.where(lane16, s_f, s_r), jnp.where(lane16, e_f, e_r)
    s_in = [jnp.where(lane16, state, e1 * state + sts[1]), jnp.where(lane16, e0 * state + sts[0], state)]
    e_out = [jnp.where(lane16, ads[1] + e1 * adj, adj), jnp.where(lane16, adj, ads[0] + e0 * adj)]
    s_out = [e0 * s_in[0] + sts[0], e1 * s_in[1] + sts[1]]

    same = ones_where((iota((128, 128), 0) < 64) == (iota((128, 128), 1) < 64))
    ii, jj = iota((CH, CH), 0), iota((CH, CH), 1)
    for c in range(2):
        rows = slice(c * CH, (c + 1) * CH)
        pre, zz, dtr, gg, cum = (r[rows, :] for r in (pre_s, z_s, dtr_s, gg_s, cum_s))
        sg, sz = sigmoid(pre), sigmoid(zz)
        xc, gate = pre * sg, zz * sz
        dt = softplus(dtr)
        u, dy = dt * xc, gg * gate
        ub, dyb = u.astype(BF), dy.astype(BF)
        rem, grow = jnp.exp(ends[c] - cum), jnp.exp(cum)
        cum_t = cum.T
        sb, eb = s_in[c].astype(BF), e_out[c].astype(BF)
        y_s, du_s, tails = [], [], []
        for s in range(2):
            bc = bc_s[s, rows, :]
            b, cc = bc[:, 0:16], bc[:, 16:32]
            col, across = cum[:, 64 * s:64 * s + 1], cum_t[64 * s:64 * s + 1, :]
            mask = (ii >= jj) if s == 0 else (ii <= jj)
            decay = jnp.exp(jnp.where(mask, col - across, -1e30))
            w = (nt(cc, b) * decay).astype(BF)
            rem_c, grow_c = rem[:, 64 * s:64 * s + 1], grow[:, 64 * s:64 * s + 1]
            y_s.append(nn(w, ub) + grow_c * nn(cc, sb))
            du_s.append(tn(w, dyb) + rem_c * nn(b, eb))
            half = lanes if s == 0 else jnp.logical_not(lanes)
            dym = jnp.where(half, dy, 0.0).astype(BF)
            um = jnp.where(half, u, 0.0).astype(BF)
            ds = (nt(dym, ub) * decay).astype(BF)
            dc = nn(ds, b) + grow_c * nt(dym, sb)
            db = tn(ds, cc) + rem_c * nt(um, eb)
            tails.append((db, dc))
        y2, du = jnp.where(lanes, y_s[0], y_s[1]), jnp.where(lanes, du_s[0], du_s[1])
        dl = exact_right(dyb.astype(F32) * y2 - ub.astype(F32) * du, same)
        direct = exact_right(du * xc, same)
        const = jnp.sum(e_out[c] * s_out[c], axis=0, keepdims=True)
        const = exact_right(jnp.broadcast_to(const, (16, 128)), same)[0:1]
        dla = jnp.where(lanes, exact_left(upp, dl), exact_left(low, dl)) + const
        ddt = (rate * dla + direct) * sigmoid(dtr)
        full = y2 + skip * xc
        gated_s[rows, :] = (full * gate).astype(BF)
        dz_s[rows, :] = gg * full * (sz * (1.0 + zz * (1.0 - sz)))
        dpre_s[rows, :] = (du * dt + skip * dy) * (sg * (1.0 + pre * (1.0 - sg)))
        for s in range(2):
            db, dc = tails[s]
            tail = jnp.concatenate([db, dc, ddt[:, 64 * s:64 * s + 1], jnp.zeros((CH, 95), F32)], axis=1).astype(BF)
            tail_s[rows, s * 128:(s + 1) * 128] = tail
            gcat[rows, s * 256 + 128:(s + 1) * 256] = tail

    go(dpre_s.at[ROWS - 8:ROWS, :], edge_s.at[0], ed_s.at[0], ed_r.at[0], yp[0])
    go(dpre_s.at[0:8, :], edge_s.at[1], ed_s.at[1], ed_r.at[1], yp[2])

    near, far = dev(x, y + 1 - 2 * lax.rem(y, 2), z, core), dev(x, 3 - y, z, core)
    turn, side = lax.rem((y + 1) // 2, 2), y // 2
    plan = ((near, turn, far, side), (far, side, near, turn))

    class Sum:
        def __init__(self, src, ref, size, b1, k1, b2, ss, rs):
            self.src, self.ref, self.size, self.b1, self.k1, self.b2, self.ss, self.rs = src, ref, size, b1, k1, b2, ss, rs

        def rows(self, k):
            return pl.ds(pl.multiple_of(k * self.size, self.size), self.size)

        def cols(self, h, k):
            return pl.ds(pl.multiple_of(h * 1024 + k * 512, 512), 512)

        def first(self):
            for h in range(2):
                p1, k1, _, _ = plan[h]
                go(self.src.at[self.rows(1 - k1), h * 1024:(h + 1) * 1024], self.b1.at[h], self.ss.at[h, 0], self.rs.at[h, 0], p1)

        def second(self):
            for h in range(2):
                _, k1, p2, k2 = plan[h]
                arrived(self.b1.at[h], self.rs.at[h, 0])
                for q in range(2):
                    c = slice(h * 1024 + q * 512, h * 1024 + (q + 1) * 512)
                    self.k1[h, q] = (self.src[self.rows(k1), c].astype(F32) + self.b1[h, :, q * 512:(q + 1) * 512].astype(F32)).astype(BF)
                go(self.k1.at[h, 1 - k2], self.b2.at[h], self.ss.at[h, 1], self.rs.at[h, 1], p2)

        def third(self):
            for h in range(2):
                _, k1, p2, k2 = plan[h]
                arrived(self.b2.at[h], self.rs.at[h, 1])
                at = (self.rows(k1), self.cols(h, k2))
                self.ref[at] = (self.k1[h, k2].astype(F32) + self.b2[h].astype(F32)).astype(BF)
                go(self.ref.at[at], self.ref.at[at], self.ss.at[h, 2], self.rs.at[h, 2], p2)

        def fourth(self):
            for h in range(2):
                p1, k1, _, k2 = plan[h]
                arrived(self.ref.at[self.rows(k1), self.cols(h, 1 - k2)], self.rs.at[h, 2])
                at = (self.rows(k1), slice(h * 1024, (h + 1) * 1024))
                go(self.ref.at[at], self.ref.at[at], self.ss.at[h, 3], self.rs.at[h, 3], p1)

        def last(self):
            for h in range(2):
                _, k1, _, _ = plan[h]
                arrived(self.ref.at[self.rows(1 - k1), h * 1024:(h + 1) * 1024], self.rs.at[h, 3])

    s_out_w = Sum(dwo, dwo_ref, 32, eo1, ko1, eo2, eo_s, eo_r)
    s_in_w = Sum(dwi, dwi_ref, 64, ei1, ki1, ei2, ei_s, ei_r)

    acc[0:128, mine] = tn(gated_s[...], own[1].reshape(ROWS, HALF))
    acc[0:128, theirs] = tn(gated_s[...], oth[1].reshape(ROWS, HALF))
    for q in range(8):
        c, back = slice(q * 256, (q + 1) * 256), slice((7 - q) * 256, (8 - q) * 256)
        dwo[:, c] = ((acc[0:64, c] + nn(acc[64:128, back].astype(BF), flip)) * SCALING).astype(BF)
    s_out_w.first()

    acc[:, mine] = tn(tail_s[...], own[0].reshape(ROWS, HALF))
    acc[:, theirs] = tn(tail_s[...], oth[0].reshape(ROWS, HALF))
    for q in range(8):
        c, back = slice(q * 256, (q + 1) * 256), slice((7 - q) * 256, (8 - q) * 256)
        wb = ((acc[0:32, c] + nn(acc[128:160, back].astype(BF), flip)) * SCALING).astype(BF)
        m = (q % 4) * 2
        fb[q // 4, m * 32:(m + 1) * 32, :] = wb[:, 0:128]
        fb[q // 4, (m + 1) * 32:(m + 2) * 32, :] = wb[:, 128:256]
    go(fb.at[1 - core], fc, fc_s.at[0], fc_r.at[0], other)

    d_scr[8:8 + ROWS, :] = dpre_s[...]
    for j in range(2):
        arrived(edge_s.at[j], ed_r.at[j])
    d_scr[0:8, :] = jnp.where(y == 0, 0.0, edge_s[0])
    d_scr[8 + ROWS:EXT, :] = jnp.where(y == 3, 0.0, edge_s[1])
    dx = taps[6] * d_scr[5:5 + ROWS, :]
    for k in range(1, 7):
        dx = dx + taps[6 - k] * d_scr[5 + k:5 + k + ROWS, :]
    dz = dz_s[...]
    lanes = fwd_lanes((ROWS, 128))
    gcat[:, 0:128] = jnp.where(lanes, dx, pltpu.roll(dz, 64, 1)).astype(BF)
    gcat[:, 256:384] = jnp.where(lanes, pltpu.roll(dx, 64, 1), dz).astype(BF)

    arrived(fc, fc_r.at[0])
    for k in range(4):
        f1[k] = (fb[core, k * 64:(k + 1) * 64, :].astype(F32) + fc[k * 64:(k + 1) * 64, :].astype(F32)).astype(BF)
    for k in (1, 2, 3):
        go(f1.at[lax.rem(x + k, 4)], fx.at[k - 1], fx_s.at[k - 1], fx_r.at[k - 1], xp[k - 1])
    s_out_w.second()

    near_rows = pl.ds(pl.multiple_of(zh * 256, 256), 256)
    g_f, g_r = gcat[near_rows, 0:256], gcat[near_rows, 256:512]
    gin[0] = (nt(g_f, wcat[theirs, :]) + nt(g_r, wf[theirs, :])).astype(BF)
    go(gin.at[0], rc, dc_s.at[0], dc_r.at[0], other)
    gin[1] = (nt(g_f, wcat[mine, :]) + nt(g_r, wf[mine, :])).astype(BF)
    for k in (1, 2, 3):
        arrived(fx.at[k - 1], fx_r.at[k - 1])
    for k in range(8):
        r = slice(k * 8, (k + 1) * 8)
        f2[k] = (f1[x, r, :].astype(F32) + fx[0, r, :].astype(F32) + fx[1, r, :].astype(F32) + fx[2, r, :].astype(F32)).astype(BF)
    for k in range(1, 8):
        go(f2.at[lax.rem(zl + k, 8)], fz.at[k - 1], fz_s.at[k - 1], fz_r.at[k - 1], line(k))
    arrived(rc, dc_r.at[0])
    for k in range(4):
        w1[k] = (gin[1, k * 64:(k + 1) * 64, :].astype(F32) + rc[k * 64:(k + 1) * 64, :].astype(F32)).astype(BF)
    for k in (2, 1, 3):
        go(w1.at[lax.rem(x + k, 4)], rx.at[k - 1], dx_s.at[k - 1], dx_r.at[k - 1], xp[k - 1])
    s_out_w.third()

    both = jnp.concatenate([gcat[:, 0:128], gcat[:, 256:384]], axis=1)
    acc[:, mine] = tn(both, own[0].reshape(ROWS, HALF))
    acc[:, theirs] = tn(both, oth[0].reshape(ROWS, HALF))
    for q in range(8):
        c, back = slice(q * 256, (q + 1) * 256), slice((7 - q) * 256, (8 - q) * 256)
        dwi[:, c] = ((acc[0:128, c] + nn(acc[128:256, back].astype(BF), flip)) * SCALING).astype(BF)
    s_in_w.first()
    s_out_w.fourth()
    for k in range(1, 8):
        arrived(fz.at[k - 1], fz_r.at[k - 1])
    part = f2[zl].astype(F32)
    for k in range(7):
        part = part + fz[k].astype(F32)
    fy[...] = part
    for k in range(3):
        go(fy, ry.at[k], fy_s.at[k], fy_r.at[k], yp[k])
    s_in_w.second()
    for k in (1, 3, 2):
        arrived(rx.at[k - 1], dx_r.at[k - 1])
    for k in range(8):
        r = slice(k * 8, (k + 1) * 8)
        w2[k] = (w1[x, r, :].astype(F32) + rx[0, r, :].astype(F32) + rx[1, r, :].astype(F32) + rx[2, r, :].astype(F32)).astype(BF)
    for k in (4, 5, 3, 6, 2, 7, 1):
        go(w2.at[lax.rem(zl + k, 8)], rz.at[k - 1], dz_ss.at[k - 1], dz_rr.at[k - 1], line(k))
    for k in range(3):
        arrived(ry.at[k], fy_r.at[k])
    at = x * 8 + zl
    fg_ref[core, at] = (fy[...] + ry[0] + ry[1] + ry[2]).astype(BF)
    for k in range(1, 8):
        go(fg_ref.at[core, at], fg_ref.at[core, at], ga_s.at[k - 1], ga_r.at[k - 1], line(k))
    s_in_w.third()
    for k in range(1, 8):
        arrived(fg_ref.at[core, x * 8 + lax.rem(zl + 8 - k, 8)], ga_r.at[k - 1])
    column = pl.ds(x * 8, 8)
    for k in (1, 2, 3):
        go(fg_ref.at[core, column], fg_ref.at[core, column], ga_s.at[6 + k], ga_r.at[6 + k], xp[k - 1])
    for k in range(1, 8):
        arrived(rz.at[k - 1], dz_rr.at[k - 1])
    hid = w2[zl].astype(F32)
    for k in range(7):
        hid = hid + rz[k].astype(F32)
    hs[...] = hid.astype(BF)
    go(hs, hr, dc_s.at[1], dc_r.at[1], other)
    s_in_w.fourth()
    for k in (1, 2, 3):
        arrived(fg_ref.at[core, pl.ds(lax.rem(x + 4 - k, 4) * 8, 8)], ga_r.at[6 + k])
    go(fg_ref.at[core], fg_ref.at[core], fc_s.at[1], fc_r.at[1], other)
    arrived(hr, dc_r.at[1])
    a, b = hs[...].astype(F32), hr[...].astype(F32)
    a, b = jnp.where(core == 0, a[0:4], a[4:8]), jnp.where(core == 0, b[0:4], b[4:8])
    hid_ref[:, 0:1024] = jnp.where(core == 0, a, b).astype(BF)
    hid_ref[:, 1024:2048] = jnp.where(core == 0, b, a).astype(BF)
    arrived(fg_ref.at[1 - core], fc_r.at[1])
    s_out_w.last()
    s_in_w.last()
    for copy in pend:
        copy.wait_send()


def mixer(*args):
    def bf(*shape):
        return pltpu.VMEM(shape, BF)

    def f32(*shape):
        return pltpu.VMEM(shape, F32)

    def sems(*shape):
        return [pltpu.SemaphoreType.DMA(shape)] * 2

    def out(*shape):
        return jax.ShapeDtypeStruct(shape, BF)

    V = pl.BlockSpec(memory_space=pltpu.VMEM)
    scratch = [
        bf(2, 4, HALF), f32(8, HALF), bf(2, 64, 8, HALF), bf(2, 64, 8, HALF), bf(2, 8, HALF), bf(2, 8, HALF),
        bf(D, 256), bf(D, 256), bf(128, D), f32(EXT, 128), f32(EXT, 128),
        f32(ROWS, 128), f32(ROWS, 128), f32(ROWS, 128), f32(ROWS, 128), bf(2, ROWS, 128), f32(ROWS, 128),
        f32(40, 128), f32(4, 40, 128), bf(ROWS, 128), f32(ROWS, 128), f32(ROWS, 128), bf(ROWS, 256), f32(2, 8, 128),
        bf(ROWS, 512), f32(256, D), bf(128, D), bf(64, D), bf(2, 256, HALF), bf(256, HALF), bf(4, 64, HALF), bf(3, 64, HALF), bf(8, 8, HALF), bf(7, 8, HALF),
        bf(8, HALF), bf(8, HALF),
        bf(2, 256, 128), bf(256, 128), bf(4, 64, 128), bf(3, 64, 128), bf(8, 8, 128), bf(7, 8, 128), f32(8, 128), f32(3, 8, 128),
        bf(2, 64, 1024), bf(2, 2, 64, 512), bf(2, 64, 512), bf(2, 32, 1024), bf(2, 2, 32, 512), bf(2, 32, 512),
        *sems(2), *sems(16), *sems(3, 16), *sems(64), *sems(2), *sems(2), *sems(3), *sems(2),
        *sems(2), *sems(3), *sems(7), *sems(2), *sems(3), *sems(7), *sems(3), *sems(10), *sems(2, 4), *sems(2, 4),
    ]
    return pl.pallas_call(
        mixer_kernel,
        out_shape=(out(4, D), out(128, D), out(64, D), out(2, 32, 8, 128)),
        in_specs=[V] * 10, out_specs=[V] * 4, scratch_shapes=scratch,
        compiler_params=pltpu.CompilerParams(collective_id=0, has_side_effects=True, vmem_limit_bytes=56 << 20),
        name="mixer",
    )(*args)


def local(hidden, w_in, w_bc, w_dt, dt_bias, a_log, d_skip, conv_w, w_out, d_out):
    one = (1, 1)
    d_hidden, dwi, dwo, shared = mixer(
        hidden, d_out, w_in, w_bc, w_dt, dt_bias.reshape(one), a_log.reshape(one), d_skip.reshape(one), conv_w, w_out
    )
    d_w_bc = shared.reshape(2, 8, 32, 128).transpose(0, 1, 3, 2).reshape(D, 2 * 16).astype(F32)
    return (d_hidden, dwi.T.astype(F32), dwo.astype(F32), d_w_bc)


def solution(mesh):
    in_specs = (
        P(("ctx", "tp"), None), P(None, "tp"), P(), P("tp", None), P("tp"), P("tp"), P("tp"), P(None, "tp"),
        P("tp", None), P(("ctx", "tp"), None),
    )
    out_specs = (P(("ctx", "tp"), None), P(None, "tp"), P("tp", None), P())
    return jax.shard_map(local, mesh=mesh, in_specs=in_specs, out_specs=out_specs, check_vma=False)
```

```python
import math

import jax
import jax.numpy as jnp
from jax import lax
from jax.experimental import pallas as pl
from jax.experimental.pallas import tpu as pltpu
from jax.sharding import PartitionSpec as P

MESH = pl.DeviceIdType.MESH
BF, F32 = jnp.bfloat16, jnp.float32
ROWS, EXT, D, HALF, CH = 512, 528, 2048, 1024, 256
SCALING = 1.0 / math.sqrt(D)


def place():
    ctx, tp = lax.axis_index("ctx"), lax.axis_index("tp")
    y, zh = ctx // 2, ctx % 2
    x, zl, core = tp // 16, (tp // 2) % 8, tp % 2
    return x, y, zh * 8 + zl, core


def dev(x, y, z, core):
    return (y * 2 + z // 8, x * 16 + (z % 8) * 2 + core)


def greet(peers):
    barrier = pltpu.get_barrier_semaphore()
    for peer in peers:
        pl.semaphore_signal(barrier, inc=1, device_id=peer, device_id_type=MESH)
    pl.semaphore_wait(barrier, len(peers))


def remote(src, dst, ssem, rsem, peer):
    return pltpu.make_async_remote_copy(src_ref=src, dst_ref=dst, send_sem=ssem, recv_sem=rsem, device_id=peer, device_id_type=MESH)


def mm(a, b, dims):
    return lax.dot_general(a, b, (dims, ((), ())), preferred_element_type=F32)


def nn(a, b):
    return mm(a, b, ((1,), (0,)))


def nt(a, b):
    return mm(a, b, ((1,), (1,)))


def tn(a, b):
    return mm(a, b, ((0,), (0,)))


def iota(shape, dim):
    return lax.broadcasted_iota(jnp.int32, shape, dim)


def ones_where(mask):
    return mask.astype(F32).astype(BF)


def split3(v):
    h = v.astype(BF)
    m = (v - h.astype(F32)).astype(BF)
    l = (v - h.astype(F32) - m.astype(F32)).astype(BF)
    return h, m, l


def exact_left(t, v):
    h, m, l = split3(v)
    return (nn(t, l) + nn(t, m)) + nn(t, h)


def exact_right(v, t):
    h, m, l = split3(v)
    return (nn(l, t) + nn(m, t)) + nn(h, t)


def fwd_lanes(shape):
    return iota(shape, 1) < 64


def softplus(v):
    return jnp.maximum(v, 0.0) + jnp.log1p(jnp.exp(-jnp.abs(v)))


def sigmoid(v):
    return jax.nn.sigmoid(v)


def mixer_kernel(h_hbm, g_hbm, win_hbm, wbc_hbm, wdt_hbm, bias_ref, alog_ref, skip_ref, conv_hbm, wout_hbm,
                 hid_ref, dwi_ref, dwo_ref, shared_ref,
                 h_ref, g_ref, win_ref, wbc_ref, wdt_ref, conv_ref, wout_ref, in_sem, swap, asm, own, oth, hown, hoth, wcat, wf, wo, x_scr, d_scr,
                 pre_s, z_s, dtr_s, gg_s, bc_s, cum_s, total_s, all_s, gated_s, dpre_s, dz_s, tail_s, edge_s,
                 gcat, acc, dwi, dwi_sum, dwo, fg, gin, rc, w1, rx, w2, rz, hs, hr,
                 fb, fc, f1, fx, f2, fz, fy, ry, ei1, ki1, ei2, eo1, ko1, eo2,
                 sw_s, sw_r, zs, zr, xs, xr, cs, cr, ys, yr, hs_s, hs_r, st_s, st_r, ed_s, ed_r,
                 dc_s, dc_r, dx_s, dx_r, dz_ss, dz_rr, fc_s, fc_r, fx_s, fx_r, fz_s, fz_r, fy_s, fy_r, ga_s, ga_r,
                 ei_s, ei_r, eo_s, eo_r):
    x, y, z, core = place()
    zh, zl = z // 8, z % 8
    bias, skip = bias_ref[0], skip_ref[0]
    rate = -jnp.exp(jnp.full((1, 128), alog_ref[0], F32))
    other = dev(x, y, z, 1 - core)
    xp = [dev(lax.rem(x + k, 4), y, z, core) for k in (1, 2, 3)]
    yp = [dev(x, lax.rem(y + k, 4), z, core) for k in (1, 2, 3)]

    def along(k):
        return dev(x, y, lax.rem(z + 16 + k, 16), core)

    def line(k):
        return dev(x, y, zh * 8 + lax.rem(zl + k, 8), core)

    mine = pl.ds(pl.multiple_of(core * HALF, HALF), HALF)
    theirs = pl.ds(pl.multiple_of((1 - core) * HALF, HALF), HALF)
    pend = []

    def go(src, dst, ssem, rsem, peer):
        copy = remote(src, dst, ssem, rsem, peer)
        copy.start()
        pend.append(copy)
        return copy

    def arrived(dst, rsem):
        remote(dst, dst, sw_s.at[0], rsem, other).wait_recv()

    loads = []
    for src, dst in ((h_hbm, h_ref), (g_hbm, g_ref), (wdt_hbm, wdt_ref), (conv_hbm, conv_ref), (wbc_hbm, wbc_ref), (win_hbm, win_ref), (wout_hbm, wout_ref)):
        loads.append(pltpu.make_async_copy(src, dst, in_sem.at[len(loads)]))
        loads[-1].start()
    greet([other] + xp + yp + [along(k) for k in (-3, -2, -1, 1, 2, 3)] + [line(k) for k in range(1, 8)])

    loads[0].wait()
    loads[1].wait()
    go(h_ref.at[:, theirs], swap.at[0], sw_s.at[0], sw_r.at[0], other)
    go(g_ref.at[:, theirs], swap.at[1], sw_s.at[1], sw_r.at[1], other)

    def blk(xx, k):
        zz = lax.rem(z + 16 + k, 16)
        return (zz // 8) * 32 + xx * 8 + zz % 8

    home = blk(x, 0)
    arrived(swap.at[0], sw_r.at[0])
    arrived(swap.at[1], sw_r.at[1])
    for k, ref in ((0, h_ref), (1, g_ref)):
        here, there = ref[:, mine].astype(F32), swap[k].astype(F32)
        asm[0:4, :] = jnp.where(core == 0, here, there)
        asm[4:8, :] = jnp.where(core == 0, there, here)
        own[k, home] = asm[...].astype(BF)

    def slot(k):
        return k if k >= 0 else 7 - k

    def cross(b, n):
        go(own.at[:, b], oth.at[:, b], cs.at[n], cr.at[n], other)

    def carry(k, far):
        b, n = blk(x, k), slot(k - far)
        go(own.at[:, b], own.at[:, b], zs.at[n], zr.at[n], along(far))

    def spread(k):
        b, n = blk(x, k), slot(k)
        go(own.at[:, b], own.at[:, b], xs.at[0, n], xr.at[0, n], xp[0])
        go(own.at[:, b], own.at[:, b], xs.at[1, n], xr.at[1, n], xp[2])
        cross(b, n)

    def z_arrival(k):
        arrived(own.at[:, blk(x, k)], zr.at[slot(k)])

    def x_arrivals(k):
        n = slot(k)
        b = blk(lax.rem(x + 3, 4), k)
        arrived(own.at[:, b], xr.at[0, n])
        go(own.at[0, b], own.at[0, b], xs.at[2, n], xr.at[2, n], xp[0])
        cross(b, 16 + n)
        b = blk(lax.rem(x + 1, 4), k)
        arrived(own.at[:, b], xr.at[1, n])
        go(own.at[1, b], own.at[1, b], xs.at[3, n], xr.at[3, n], xp[2])
        cross(b, 32 + n)

    def far_arrival(k):
        n, b = slot(k), blk(lax.rem(x + 2, 4), k)
        arrived(own.at[0, b], xr.at[2, n])
        arrived(own.at[1, b], xr.at[3, n])
        cross(b, 48 + n)

    for far in (3, -3, 2, -2, 1, -1):
        carry(0, far)
    spread(0)

    for copy in loads[2:]:
        copy.wait()
    flip = ones_where(iota((256, 256), 0) + iota((256, 256), 1) == 255)
    pick = ones_where((iota((40, 128), 1) == iota((40, 128), 0)) & (iota((40, 128), 0) < 33))
    for q in range(8):
        r, back = slice(q * 256, (q + 1) * 256), slice((7 - q) * 256, (8 - q) * 256)
        wcat[r, 0:128] = win_ref[r, :]
        shared = jnp.concatenate([wbc_ref[:, r].astype(F32), jnp.broadcast_to(wdt_ref[:, r].astype(F32), (8, 256))], axis=0)
        wcat[r, 128:256] = tn(shared.astype(BF), pick).astype(BF)
        wo[0:64, r] = wout_ref[:, r]
        wo[64:128, r] = nn(wout_ref[:, back], flip).astype(BF)
    for q in range(8):
        wf[q * 256:(q + 1) * 256, :] = nn(flip, wcat[(7 - q) * 256:(8 - q) * 256, :]).astype(BF)
    gap = jnp.zeros((1, 64), F32)
    taps = []
    for k in range(7):
        f_tap = conv_ref[k:k + 1, :] if k < 4 else gap
        r_tap = conv_ref[6 - k:7 - k, :] if k >= 3 else gap
        taps.append(jnp.concatenate([f_tap, r_tap], axis=1))

    for k in (-3, 3):
        z_arrival(k)
        for far in (3, 2, 1):
            carry(k, far if k < 0 else -far)
    for k in (-1, 1, -2, 2):
        z_arrival(k)
        spread(k)
    spread(-3)
    spread(3)
    x_arrivals(0)
    z_arrival(-6)
    carry(-6, 2)
    carry(-6, 1)
    z_arrival(6)
    carry(6, -1)
    for k in (-1, 1, -2, 2, -3, 3):
        x_arrivals(k)
    for k in (-4, 4, -5, 5):
        z_arrival(k)
        spread(k)
    spread(-6)
    spread(6)
    far_arrival(0)
    for k in (-7, 7, -8):
        z_arrival(k)
        spread(k)
    for k in (-4, 4, -5, 5, -6, 6):
        x_arrivals(k)
    for k in (-1, 1, -2, 2, -3, 3):
        far_arrival(k)
    for k in (-7, 7, -8):
        x_arrivals(k)
    for k in (-4, 4, -5, 5, -6, 6, -7, 7, -8):
        far_arrival(k)
    go(own.at[0, 63], hown.at[0], ys.at[0], yr.at[0], yp[0])
    go(own.at[0, 0], hown.at[1], ys.at[1], yr.at[1], yp[2])
    for n in range(64):
        arrived(oth.at[:, 0], cr.at[n])

    h_own, h_oth = own[0].reshape(ROWS, HALF), oth[0].reshape(ROWS, HALF)
    g_own, g_oth = own[1].reshape(ROWS, HALF), oth[1].reshape(ROWS, HALF)
    gg = nt(g_own, wo[:, mine]) + nt(g_oth, wo[:, theirs])
    gg_s[...] = gg
    for j in range(2):
        arrived(hown.at[j], yr.at[j])
        go(hown.at[j], hoth.at[j], hs_s.at[j], hs_r.at[j], other)
    pf = nn(h_own, wcat[mine, :]) + nn(h_oth, wcat[theirs, :])
    pr = nn(h_own, wf[mine, :]) + nn(h_oth, wf[theirs, :])
    lanes = fwd_lanes((ROWS, 128))
    x2 = jnp.where(lanes, pf[:, 0:128], pltpu.roll(pr[:, 0:128], 64, 1)).astype(BF).astype(F32)
    z2 = jnp.where(lanes, pltpu.roll(pf[:, 0:128], 64, 1), pr[:, 0:128]).astype(BF).astype(F32)
    x_scr[8:8 + ROWS, :] = x2
    z_s[...] = z2
    bf, br = pf[:, 128:256], pr[:, 128:256]
    bc_s[0] = bf.astype(BF)
    bc_s[1] = br.astype(BF)
    dtr = jnp.where(lanes, bf[:, 32:33], br[:, 32:33]) + bias
    dtr_s[...] = dtr
    dt = softplus(dtr)
    la = dt * rate
    dy = gg * (z2 * sigmoid(z2))
    for j in range(2):
        arrived(hoth.at[j], hs_r.at[j])
    e_own, e_oth = hown[...].reshape(16, HALF), hoth[...].reshape(16, HALF)
    xf = nn(e_own, wcat[mine, 0:128]) + nn(e_oth, wcat[theirs, 0:128])
    xb = nn(e_own, wf[mine, 0:128]) + nn(e_oth, wf[theirs, 0:128])
    edge = jnp.where(fwd_lanes((16, 128)), xf, pltpu.roll(xb, 64, 1)).astype(BF).astype(F32)
    x_scr[0:8, :] = jnp.where(y == 0, 0.0, edge[0:8])
    x_scr[8 + ROWS:EXT, :] = jnp.where(y == 3, 0.0, edge[8:16])
    pre = taps[0] * x_scr[5:5 + ROWS, :]
    for k in range(1, 7):
        pre = pre + taps[k] * x_scr[5 + k:5 + k + ROWS, :]
    pre_s[...] = pre
    u = dt * (pre * sigmoid(pre))

    low = ones_where(iota((CH, CH), 0) >= iota((CH, CH), 1))
    upp = ones_where(iota((CH, CH), 0) <= iota((CH, CH), 1))
    lanes, lane1, lane16 = fwd_lanes((CH, 128)), fwd_lanes((1, 128)), fwd_lanes((16, 128))
    ends, sts, ads = [], [], []
    for c in range(2):
        rows = slice(c * CH, (c + 1) * CH)
        cum = jnp.where(lanes, exact_left(low, la[rows]), exact_left(upp, la[rows]))
        cum_s[rows, :] = cum
        end = jnp.where(lane1, cum[CH - 1:CH], cum[0:1])
        ru = (jnp.exp(end - cum) * u[rows]).astype(BF)
        ed = (jnp.exp(cum) * dy[rows]).astype(BF)
        b0, b1 = bf[rows].astype(BF), br[rows].astype(BF)
        sts.append(jnp.where(lane16, tn(b0, ru)[0:16], tn(b1, ru)[0:16]))
        ads.append(jnp.where(lane16, tn(b0, ed)[16:32], tn(b1, ed)[16:32]))
        ends.append(end)
    e0, e1 = jnp.exp(ends[0]), jnp.exp(ends[1])
    total_s[0:16, :] = jnp.where(lane16, e1 * sts[0] + sts[1], e0 * sts[1] + sts[0])
    total_s[16:32, :] = jnp.where(lane16, ads[0] + e0 * ads[1], ads[1] + e1 * ads[0])
    total_s[32:40, :] = jnp.broadcast_to(jnp.exp(ends[0] + ends[1]), (8, 128))
    all_s[y] = total_s[...]
    for k in range(3):
        go(total_s, all_s.at[y], st_s.at[k], st_r.at[k], yp[k])
    for k in range(3):
        arrived(all_s.at[lax.rem(y + 3 - k, 4)], st_r.at[k])
    nil = jnp.zeros((16, 128), F32)
    s_f, s_r, e_f, e_r = nil, nil, nil, nil
    for k in range(4):
        st, ad, dk = all_s[k, 0:16, :], all_s[k, 16:32, :], all_s[k, 32:33, :]
        s_f = jnp.where(k < y, dk * s_f + st, s_f)
        e_r = jnp.where(k < y, dk * e_r + ad, e_r)
    for k in (3, 2, 1, 0):
        st, ad, dk = all_s[k, 0:16, :], all_s[k, 16:32, :], all_s[k, 32:33, :]
        s_r = jnp.where(k > y, dk * s_r + st, s_r)
        e_f = jnp.where(k > y, dk * e_f + ad, e_f)
    state, adj = jnp.where(lane16, s_f, s_r), jnp.where(lane16, e_f, e_r)
    s_in = [jnp.where(lane16, state, e1 * state + sts[1]), jnp.where(lane16, e0 * state + sts[0], state)]
    e_out = [jnp.where(lane16, ads[1] + e1 * adj, adj), jnp.where(lane16, adj, ads[0] + e0 * adj)]
    s_out = [e0 * s_in[0] + sts[0], e1 * s_in[1] + sts[1]]

    same = ones_where((iota((128, 128), 0) < 64) == (iota((128, 128), 1) < 64))
    ii, jj = iota((CH, CH), 0), iota((CH, CH), 1)
    for c in range(2):
        rows = slice(c * CH, (c + 1) * CH)
        pre, zz, dtr, gg, cum = (r[rows, :] for r in (pre_s, z_s, dtr_s, gg_s, cum_s))
        sg, sz = sigmoid(pre), sigmoid(zz)
        xc, gate = pre * sg, zz * sz
        dt = softplus(dtr)
        u, dy = dt * xc, gg * gate
        ub, dyb = u.astype(BF), dy.astype(BF)
        rem, grow = jnp.exp(ends[c] - cum), jnp.exp(cum)
        cum_t = cum.T
        sb, eb = s_in[c].astype(BF), e_out[c].astype(BF)
        y_s, du_s, tails = [], [], []
        for s in range(2):
            bc = bc_s[s, rows, :]
            b, cc = bc[:, 0:16], bc[:, 16:32]
            col, across = cum[:, 64 * s:64 * s + 1], cum_t[64 * s:64 * s + 1, :]
            mask = (ii >= jj) if s == 0 else (ii <= jj)
            decay = jnp.exp(jnp.where(mask, col - across, -1e30))
            w = (nt(cc, b) * decay).astype(BF)
            rem_c, grow_c = rem[:, 64 * s:64 * s + 1], grow[:, 64 * s:64 * s + 1]
            y_s.append(nn(w, ub) + grow_c * nn(cc, sb))
            du_s.append(tn(w, dyb) + rem_c * nn(b, eb))
            half = lanes if s == 0 else jnp.logical_not(lanes)
            dym = jnp.where(half, dy, 0.0).astype(BF)
            um = jnp.where(half, u, 0.0).astype(BF)
            ds = (nt(dym, ub) * decay).astype(BF)
            dc = nn(ds, b) + grow_c * nt(dym, sb)
            db = tn(ds, cc) + rem_c * nt(um, eb)
            tails.append((db, dc))
        y2, du = jnp.where(lanes, y_s[0], y_s[1]), jnp.where(lanes, du_s[0], du_s[1])
        dl = exact_right(dyb.astype(F32) * y2 - ub.astype(F32) * du, same)
        direct = exact_right(du * xc, same)
        const = jnp.sum(e_out[c] * s_out[c], axis=0, keepdims=True)
        const = exact_right(jnp.broadcast_to(const, (16, 128)), same)[0:1]
        dla = jnp.where(lanes, exact_left(upp, dl), exact_left(low, dl)) + const
        ddt = (rate * dla + direct) * sigmoid(dtr)
        full = y2 + skip * xc
        gated_s[rows, :] = (full * gate).astype(BF)
        dz_s[rows, :] = gg * full * (sz * (1.0 + zz * (1.0 - sz)))
        dpre_s[rows, :] = (du * dt + skip * dy) * (sg * (1.0 + pre * (1.0 - sg)))
        for s in range(2):
            db, dc = tails[s]
            tail = jnp.concatenate([db, dc, ddt[:, 64 * s:64 * s + 1], jnp.zeros((CH, 95), F32)], axis=1).astype(BF)
            tail_s[rows, s * 128:(s + 1) * 128] = tail
            gcat[rows, s * 256 + 128:(s + 1) * 256] = tail

    go(dpre_s.at[ROWS - 8:ROWS, :], edge_s.at[0], ed_s.at[0], ed_r.at[0], yp[0])
    go(dpre_s.at[0:8, :], edge_s.at[1], ed_s.at[1], ed_r.at[1], yp[2])

    near, far = dev(x, y + 1 - 2 * lax.rem(y, 2), z, core), dev(x, 3 - y, z, core)
    turn, side = lax.rem((y + 1) // 2, 2), y // 2
    plan = ((near, turn, far, side), (far, side, near, turn))

    class Sum:
        def __init__(self, src, ref, size, b1, k1, b2, ss, rs):
            self.src, self.ref, self.size, self.b1, self.k1, self.b2, self.ss, self.rs = src, ref, size, b1, k1, b2, ss, rs

        def rows(self, k):
            return pl.ds(pl.multiple_of(k * self.size, self.size), self.size)

        def cols(self, h, k):
            return pl.ds(pl.multiple_of(h * 1024 + k * 512, 512), 512)

        def first(self):
            for h in range(2):
                p1, k1, _, _ = plan[h]
                go(self.src.at[self.rows(1 - k1), h * 1024:(h + 1) * 1024], self.b1.at[h], self.ss.at[h, 0], self.rs.at[h, 0], p1)

        def second(self):
            for h in range(2):
                _, k1, p2, k2 = plan[h]
                arrived(self.b1.at[h], self.rs.at[h, 0])
                for q in range(2):
                    c = slice(h * 1024 + q * 512, h * 1024 + (q + 1) * 512)
                    self.k1[h, q] = (self.src[self.rows(k1), c].astype(F32) + self.b1[h, :, q * 512:(q + 1) * 512].astype(F32)).astype(BF)
                go(self.k1.at[h, 1 - k2], self.b2.at[h], self.ss.at[h, 1], self.rs.at[h, 1], p2)

        def third(self):
            for h in range(2):
                _, k1, p2, k2 = plan[h]
                arrived(self.b2.at[h], self.rs.at[h, 1])
                at = (self.rows(k1), self.cols(h, k2))
                self.ref[at] = (self.k1[h, k2].astype(F32) + self.b2[h].astype(F32)).astype(BF)
                go(self.ref.at[at], self.ref.at[at], self.ss.at[h, 2], self.rs.at[h, 2], p2)

        def fourth(self):
            for h in range(2):
                p1, k1, _, k2 = plan[h]
                arrived(self.ref.at[self.rows(k1), self.cols(h, 1 - k2)], self.rs.at[h, 2])
                at = (self.rows(k1), slice(h * 1024, (h + 1) * 1024))
                go(self.ref.at[at], self.ref.at[at], self.ss.at[h, 3], self.rs.at[h, 3], p1)

        def last(self):
            for h in range(2):
                _, k1, _, _ = plan[h]
                arrived(self.ref.at[self.rows(1 - k1), h * 1024:(h + 1) * 1024], self.rs.at[h, 3])

    s_out_w = Sum(dwo, dwo_ref, 32, eo1, ko1, eo2, eo_s, eo_r)
    s_in_w = Sum(dwi, dwi_sum, 64, ei1, ki1, ei2, ei_s, ei_r)

    acc[0:128, mine] = tn(gated_s[...], own[1].reshape(ROWS, HALF))
    acc[0:128, theirs] = tn(gated_s[...], oth[1].reshape(ROWS, HALF))
    for q in range(8):
        c, back = slice(q * 256, (q + 1) * 256), slice((7 - q) * 256, (8 - q) * 256)
        dwo[:, c] = ((acc[0:64, c] + nn(acc[64:128, back].astype(BF), flip)) * SCALING).astype(BF)
    s_out_w.first()

    acc[:, mine] = tn(tail_s[...], own[0].reshape(ROWS, HALF))
    acc[:, theirs] = tn(tail_s[...], oth[0].reshape(ROWS, HALF))
    for q in range(8):
        c, back = slice(q * 256, (q + 1) * 256), slice((7 - q) * 256, (8 - q) * 256)
        wb = ((acc[0:32, c] + nn(acc[128:160, back].astype(BF), flip)) * SCALING).astype(BF)
        m = (q % 4) * 2
        fb[q // 4, m * 32:(m + 1) * 32, :] = wb[:, 0:128]
        fb[q // 4, (m + 1) * 32:(m + 2) * 32, :] = wb[:, 128:256]
    go(fb.at[1 - core], fc, fc_s.at[0], fc_r.at[0], other)

    d_scr[8:8 + ROWS, :] = dpre_s[...]
    for j in range(2):
        arrived(edge_s.at[j], ed_r.at[j])
    d_scr[0:8, :] = jnp.where(y == 0, 0.0, edge_s[0])
    d_scr[8 + ROWS:EXT, :] = jnp.where(y == 3, 0.0, edge_s[1])
    dx = taps[6] * d_scr[5:5 + ROWS, :]
    for k in range(1, 7):
        dx = dx + taps[6 - k] * d_scr[5 + k:5 + k + ROWS, :]
    dz = dz_s[...]
    lanes = fwd_lanes((ROWS, 128))
    gcat[:, 0:128] = jnp.where(lanes, dx, pltpu.roll(dz, 64, 1)).astype(BF)
    gcat[:, 256:384] = jnp.where(lanes, pltpu.roll(dx, 64, 1), dz).astype(BF)

    arrived(fc, fc_r.at[0])
    for k in range(4):
        f1[k] = (fb[core, k * 64:(k + 1) * 64, :].astype(F32) + fc[k * 64:(k + 1) * 64, :].astype(F32)).astype(BF)
    for k in (1, 2, 3):
        go(f1.at[lax.rem(x + k, 4)], fx.at[k - 1], fx_s.at[k - 1], fx_r.at[k - 1], xp[k - 1])
    s_out_w.second()

    near_rows = pl.ds(pl.multiple_of(zh * 256, 256), 256)
    g_f, g_r = gcat[near_rows, 0:256], gcat[near_rows, 256:512]
    for who in range(2):
        for j in range(2):
            c = pl.ds(pl.multiple_of((core if who else 1 - core) * HALF + j * 512, 512), 512)
            gin[who, j] = (nt(g_f, wcat[c, :]) + nt(g_r, wf[c, :])).astype(BF)
            if who == 0:
                go(gin.at[0, j], rc.at[j], dc_s.at[j], dc_r.at[j], other)
    for k in (1, 2, 3):
        arrived(fx.at[k - 1], fx_r.at[k - 1])
    for k in range(8):
        r = slice(k * 8, (k + 1) * 8)
        f2[k] = (f1[x, r, :].astype(F32) + fx[0, r, :].astype(F32) + fx[1, r, :].astype(F32) + fx[2, r, :].astype(F32)).astype(BF)
    for k in range(1, 8):
        go(f2.at[lax.rem(zl + k, 8)], fz.at[k - 1], fz_s.at[k - 1], fz_r.at[k - 1], line(k))
    for j in range(2):
        arrived(rc.at[j], dc_r.at[j])
        for k in range(4):
            r = slice(k * 64, (k + 1) * 64)
            w1[j, k] = (gin[1, j, r, :].astype(F32) + rc[j, r, :].astype(F32)).astype(BF)
        for k in (2, 1, 3):
            go(w1.at[j, lax.rem(x + k, 4)], rx.at[j, k - 1], dx_s.at[j, k - 1], dx_r.at[j, k - 1], xp[k - 1])
    s_out_w.third()

    both = jnp.concatenate([gcat[:, 0:128], gcat[:, 256:384]], axis=1)
    acc[:, mine] = tn(both, own[0].reshape(ROWS, HALF))
    acc[:, theirs] = tn(both, oth[0].reshape(ROWS, HALF))
    for q in range(8):
        c, back = slice(q * 256, (q + 1) * 256), slice((7 - q) * 256, (8 - q) * 256)
        dwi[:, c] = ((acc[0:128, c] + nn(acc[128:256, back].astype(BF), flip)) * SCALING).astype(BF)
    s_in_w.first()
    s_out_w.fourth()
    for k in range(1, 8):
        arrived(fz.at[k - 1], fz_r.at[k - 1])
    part = f2[zl].astype(F32)
    for k in range(7):
        part = part + fz[k].astype(F32)
    fy[...] = part
    for k in range(3):
        go(fy, ry.at[k], fy_s.at[k], fy_r.at[k], yp[k])
    s_in_w.second()
    for j in range(2):
        for k in (1, 3, 2):
            arrived(rx.at[j, k - 1], dx_r.at[j, k - 1])
        for k in range(8):
            r = slice(k * 8, (k + 1) * 8)
            w2[j, k] = (w1[j, x, r, :].astype(F32) + rx[j, 0, r, :].astype(F32) + rx[j, 1, r, :].astype(F32) + rx[j, 2, r, :].astype(F32)).astype(BF)
        for k in (4, 5, 3, 6, 2, 7, 1):
            go(w2.at[j, lax.rem(zl + k, 8)], rz.at[j, k - 1], dz_ss.at[j, k - 1], dz_rr.at[j, k - 1], line(k))
    for k in range(3):
        arrived(ry.at[k], fy_r.at[k])
    at = x * 8 + zl
    fg[core, at] = (fy[...] + ry[0] + ry[1] + ry[2]).astype(BF)
    for k in range(1, 8):
        go(fg.at[core, at], fg.at[core, at], ga_s.at[k - 1], ga_r.at[k - 1], line(k))
    s_in_w.third()
    for k in range(1, 8):
        arrived(fg.at[core, x * 8 + lax.rem(zl + 8 - k, 8)], ga_r.at[k - 1])
    column = pl.ds(x * 8, 8)
    for k in (1, 2, 3):
        go(fg.at[core, column], fg.at[core, column], ga_s.at[6 + k], ga_r.at[6 + k], xp[k - 1])
    for j in range(2):
        for k in range(1, 8):
            arrived(rz.at[j, k - 1], dz_rr.at[j, k - 1])
        hid = w2[j, zl].astype(F32)
        for k in range(7):
            hid = hid + rz[j, k].astype(F32)
        hs[:, j * 512:(j + 1) * 512] = hid.astype(BF)
    go(hs, hr, dc_s.at[2], dc_r.at[2], other)
    s_in_w.fourth()
    for k in (1, 2, 3):
        arrived(fg.at[core, pl.ds(lax.rem(x + 4 - k, 4) * 8, 8)], ga_r.at[6 + k])
    go(fg.at[core], fg.at[core], fc_s.at[1], fc_r.at[1], other)
    arrived(hr, dc_r.at[2])
    a, b = hs[...].astype(F32), hr[...].astype(F32)
    a, b = jnp.where(core == 0, a[0:4], a[4:8]), jnp.where(core == 0, b[0:4], b[4:8])
    hid_ref[:, 0:1024] = jnp.where(core == 0, a, b).astype(BF)
    hid_ref[:, 1024:2048] = jnp.where(core == 0, b, a).astype(BF)
    arrived(fg.at[1 - core], fc_r.at[1])
    for k in range(2):
        for m in range(8):
            c = slice(k * HALF + m * 128, k * HALF + (m + 1) * 128)
            for n in range(4):
                shared_ref[n * 8:(n + 1) * 8, c] = fg[k, m * 4 + n]
    s_out_w.last()
    s_in_w.last()
    for q in range(16):
        r = slice(q * 128, (q + 1) * 128)
        dwi_ref[r, :] = dwi_sum[:, r].astype(F32).T.astype(BF)
    for copy in pend:
        copy.wait_send()


def mixer(*args):
    def bf(*shape):
        return pltpu.VMEM(shape, BF)

    def f32(*shape):
        return pltpu.VMEM(shape, F32)

    def sems(*shape):
        return [pltpu.SemaphoreType.DMA(shape)] * 2

    def out(*shape):
        return jax.ShapeDtypeStruct(shape, BF)

    V, A = pl.BlockSpec(memory_space=pltpu.VMEM), pl.BlockSpec(memory_space=pl.ANY)
    scratch = [
        bf(4, D), bf(4, D), bf(D, 128), bf(32, D), bf(1, D), f32(4, 64), bf(64, D), pltpu.SemaphoreType.DMA((7,)),
        bf(2, 4, HALF), f32(8, HALF), bf(2, 64, 8, HALF), bf(2, 64, 8, HALF), bf(2, 8, HALF), bf(2, 8, HALF),
        bf(D, 256), bf(D, 256), bf(128, D), f32(EXT, 128), f32(EXT, 128),
        f32(ROWS, 128), f32(ROWS, 128), f32(ROWS, 128), f32(ROWS, 128), bf(2, ROWS, 128), f32(ROWS, 128),
        f32(40, 128), f32(4, 40, 128), bf(ROWS, 128), f32(ROWS, 128), f32(ROWS, 128), bf(ROWS, 256), f32(2, 8, 128),
        bf(ROWS, 512), f32(256, D), bf(128, D), bf(128, D), bf(64, D), bf(2, 32, 8, 128), bf(2, 2, 256, 512), bf(2, 256, 512), bf(2, 4, 64, 512), bf(2, 3, 64, 512), bf(2, 8, 8, 512), bf(2, 7, 8, 512),
        bf(8, HALF), bf(8, HALF),
        bf(2, 256, 128), bf(256, 128), bf(4, 64, 128), bf(3, 64, 128), bf(8, 8, 128), bf(7, 8, 128), f32(8, 128), f32(3, 8, 128),
        bf(2, 64, 1024), bf(2, 2, 64, 512), bf(2, 64, 512), bf(2, 32, 1024), bf(2, 2, 32, 512), bf(2, 32, 512),
        *sems(2), *sems(16), *sems(4, 16), *sems(64), *sems(2), *sems(2), *sems(3), *sems(2),
        *sems(3), *sems(2, 3), *sems(2, 7), *sems(2), *sems(3), *sems(7), *sems(3), *sems(10), *sems(2, 4), *sems(2, 4),
    ]
    return pl.pallas_call(
        mixer_kernel,
        out_shape=(out(4, D), out(D, 128), out(64, D), out(32, D)),
        in_specs=[A] * 5 + [pl.BlockSpec(memory_space=pltpu.SMEM)] * 3 + [A] * 2, out_specs=[V] * 4, scratch_shapes=scratch,
        compiler_params=pltpu.CompilerParams(collective_id=0, has_side_effects=True, vmem_limit_bytes=56 << 20),
        name="mixer",
    )(*args)


def widen_kernel(*refs):
    sources, results, held, wide, sem_in, sem_out = refs[0:4], refs[4:8], refs[8:12], refs[12:16], refs[16], refs[17]
    ins = [pltpu.make_async_copy(sources[k], held[k], sem_in.at[k]) for k in range(4)]
    for copy in ins:
        copy.start()
    outs = []
    for k in (1, 2, 3, 0):
        ins[k].wait()
        wide[k][...] = held[k][...].astype(wide[k].dtype)
        outs.append(pltpu.make_async_copy(wide[k], results[k], sem_out.at[k]))
        outs[-1].start()
    for copy in outs:
        copy.wait()


def widen(*args):
    A = pl.BlockSpec(memory_space=pl.ANY)
    types = (BF, F32, F32, F32)
    return pl.pallas_call(
        widen_kernel,
        out_shape=tuple(jax.ShapeDtypeStruct(a.shape, t) for a, t in zip(args, types)),
        in_specs=[A] * 4, out_specs=[A] * 4,
        scratch_shapes=[pltpu.VMEM(a.shape, BF) for a in args] + [pltpu.VMEM(a.shape, t) for a, t in zip(args, types)]
        + [pltpu.SemaphoreType.DMA((4,))] * 2,
        compiler_params=pltpu.CompilerParams(vmem_limit_bytes=56 << 20),
        name="widen",
    )(*args)


def local(hidden, w_in, w_bc, w_dt, dt_bias, a_log, d_skip, conv_w, w_out, d_out):
    d_hidden, dwi, dwo, shared = mixer(hidden, d_out, w_in, w_bc.T, w_dt, dt_bias, a_log, d_skip, conv_w, w_out)
    d_hidden, d_w_in, d_w_out, d_w_bc = widen(d_hidden, dwi, dwo, shared)
    return (d_hidden, d_w_in, d_w_out, d_w_bc.T)


def solution(mesh):
    in_specs = (
        P(("ctx", "tp"), None), P(None, "tp"), P(), P("tp", None), P("tp"), P("tp"), P("tp"), P(None, "tp"),
        P("tp", None), P(("ctx", "tp"), None),
    )
    out_specs = (P(("ctx", "tp"), None), P(None, "tp"), P("tp", None), P())
    return jax.shard_map(local, mesh=mesh, in_specs=in_specs, out_specs=out_specs, check_vma=False)
```

```python
import math

import jax
import jax.numpy as jnp
from jax import lax
from jax.experimental import pallas as pl
from jax.experimental.pallas import tpu as pltpu
from jax.sharding import PartitionSpec as P

MESH = pl.DeviceIdType.MESH
BF, F32 = jnp.bfloat16, jnp.float32
ROWS, EXT, D, HALF, CH = 512, 528, 2048, 1024, 256
SCALING = 1.0 / math.sqrt(D)


def place():
    ctx, tp = lax.axis_index("ctx"), lax.axis_index("tp")
    y, zh = ctx // 2, ctx % 2
    x, zl, core = tp // 16, (tp // 2) % 8, tp % 2
    return x, y, zh * 8 + zl, core


def dev(x, y, z, core):
    return (y * 2 + z // 8, x * 16 + (z % 8) * 2 + core)


def greet(peers):
    barrier = pltpu.get_barrier_semaphore()
    for peer in peers:
        pl.semaphore_signal(barrier, inc=1, device_id=peer, device_id_type=MESH)
    pl.semaphore_wait(barrier, len(peers))


def remote(src, dst, ssem, rsem, peer):
    return pltpu.make_async_remote_copy(src_ref=src, dst_ref=dst, send_sem=ssem, recv_sem=rsem, device_id=peer, device_id_type=MESH)


def mm(a, b, dims):
    return lax.dot_general(a, b, (dims, ((), ())), preferred_element_type=F32)


def nn(a, b):
    return mm(a, b, ((1,), (0,)))


def nt(a, b):
    return mm(a, b, ((1,), (1,)))


def tn(a, b):
    return mm(a, b, ((0,), (0,)))


def iota(shape, dim):
    return lax.broadcasted_iota(jnp.int32, shape, dim)


def ones_where(mask):
    return mask.astype(F32).astype(BF)


def split3(v):
    h = v.astype(BF)
    m = (v - h.astype(F32)).astype(BF)
    l = (v - h.astype(F32) - m.astype(F32)).astype(BF)
    return h, m, l


def exact_left(t, v):
    h, m, l = split3(v)
    return (nn(t, l) + nn(t, m)) + nn(t, h)


def exact_right(v, t):
    h, m, l = split3(v)
    return (nn(l, t) + nn(m, t)) + nn(h, t)


def fwd_lanes(shape):
    return iota(shape, 1) < 64


def softplus(v):
    return jnp.maximum(v, 0.0) + jnp.log1p(jnp.exp(-jnp.abs(v)))


def sigmoid(v):
    return jax.nn.sigmoid(v)


def mixer_kernel(h_hbm, g_hbm, win_hbm, wbc_hbm, wdt_hbm, bias_ref, alog_ref, skip_ref, conv_hbm, wout_hbm,
                 hid_ref, dwi_ref, dwo_ref, shared_ref,
                 h_ref, g_ref, win_ref, wbc_ref, wdt_ref, conv_ref, wout_ref, in_sem, swap, asm, own, oth, hown, hoth, wcat, wf, wo, x_scr, d_scr,
                 pre_s, z_s, dtr_s, gg_s, bc_s, cum_s, total_s, all_s, gated_s, dpre_s, dz_s, tail_s, edge_s,
                 gcat, acc, dwx, dwx_sum, dwz, dwz_sum, dwo, fg, gin, rc, w1, rx, w2, rz, hs, hr,
                 fb, fc, f1, fx, f2, fz, ei1, ki1, ei2, ez1, kz1, ez2, eo1, ko1, eo2,
                 sw_s, sw_r, zs, zr, xs, xr, cs, cr, ys, yr, hs_s, hs_r, st_s, st_r, ed_s, ed_r,
                 dc_s, dc_r, dx_s, dx_r, dz_ss, dz_rr, fc_s, fc_r, fx_s, fx_r, fz_s, fz_r, ga_s, ga_r,
                 ei_s, ei_r, ez_s, ez_r, eo_s, eo_r):
    x, y, z, core = place()
    zh, zl = z // 8, z % 8
    bias, skip = bias_ref[0], skip_ref[0]
    rate = -jnp.exp(jnp.full((1, 128), alog_ref[0], F32))
    other = dev(x, y, z, 1 - core)
    xp = [dev(lax.rem(x + k, 4), y, z, core) for k in (1, 2, 3)]
    yp = [dev(x, lax.rem(y + k, 4), z, core) for k in (1, 2, 3)]
    steps = [(k // 4, k % 4) for k in range(1, 16)]
    plane = [dev(lax.rem(x + i, 4), lax.rem(y + j, 4), z, core) for i, j in steps]

    def along(k):
        return dev(x, y, lax.rem(z + 16 + k, 16), core)

    def line(k):
        return dev(x, y, zh * 8 + lax.rem(zl + k, 8), core)

    mine = pl.ds(pl.multiple_of(core * HALF, HALF), HALF)
    theirs = pl.ds(pl.multiple_of((1 - core) * HALF, HALF), HALF)
    pend = []

    def go(src, dst, ssem, rsem, peer):
        copy = remote(src, dst, ssem, rsem, peer)
        copy.start()
        pend.append(copy)
        return copy

    def arrived(dst, rsem):
        remote(dst, dst, sw_s.at[0], rsem, other).wait_recv()

    loads = []
    for src, dst in ((h_hbm, h_ref), (g_hbm, g_ref), (wdt_hbm, wdt_ref), (conv_hbm, conv_ref), (wbc_hbm, wbc_ref), (win_hbm, win_ref), (wout_hbm, wout_ref)):
        loads.append(pltpu.make_async_copy(src, dst, in_sem.at[len(loads)]))
        loads[-1].start()
    greet([other] + plane + [along(k) for k in (-3, -2, -1, 1, 2, 3)] + [line(k) for k in range(1, 8)])

    loads[0].wait()
    loads[1].wait()
    go(h_ref.at[:, theirs], swap.at[0], sw_s.at[0], sw_r.at[0], other)
    go(g_ref.at[:, theirs], swap.at[1], sw_s.at[1], sw_r.at[1], other)

    def blk(xx, k):
        zz = lax.rem(z + 16 + k, 16)
        return (zz // 8) * 32 + xx * 8 + zz % 8

    home = blk(x, 0)
    arrived(swap.at[0], sw_r.at[0])
    arrived(swap.at[1], sw_r.at[1])
    for k, ref in ((0, h_ref), (1, g_ref)):
        here, there = ref[:, mine].astype(F32), swap[k].astype(F32)
        asm[0:4, :] = jnp.where(core == 0, here, there)
        asm[4:8, :] = jnp.where(core == 0, there, here)
        own[k, home] = asm[...].astype(BF)

    def slot(k):
        return k if k >= 0 else 7 - k

    def cross(b, n):
        go(own.at[:, b], oth.at[:, b], cs.at[n], cr.at[n], other)

    def carry(k, far):
        b, n = blk(x, k), slot(k - far)
        go(own.at[:, b], own.at[:, b], zs.at[n], zr.at[n], along(far))

    def spread(k):
        b, n = blk(x, k), slot(k)
        go(own.at[:, b], own.at[:, b], xs.at[0, n], xr.at[0, n], xp[0])
        go(own.at[:, b], own.at[:, b], xs.at[1, n], xr.at[1, n], xp[2])
        cross(b, n)

    def z_arrival(k):
        arrived(own.at[:, blk(x, k)], zr.at[slot(k)])

    def x_arrivals(k):
        n = slot(k)
        b = blk(lax.rem(x + 3, 4), k)
        arrived(own.at[:, b], xr.at[0, n])
        go(own.at[0, b], own.at[0, b], xs.at[2, n], xr.at[2, n], xp[0])
        cross(b, 16 + n)
        b = blk(lax.rem(x + 1, 4), k)
        arrived(own.at[:, b], xr.at[1, n])
        go(own.at[1, b], own.at[1, b], xs.at[3, n], xr.at[3, n], xp[2])
        cross(b, 32 + n)

    def far_arrival(k):
        n, b = slot(k), blk(lax.rem(x + 2, 4), k)
        arrived(own.at[0, b], xr.at[2, n])
        arrived(own.at[1, b], xr.at[3, n])
        cross(b, 48 + n)

    for far in (3, -3, 2, -2, 1, -1):
        carry(0, far)
    spread(0)

    for copy in loads[2:]:
        copy.wait()
    flip = ones_where(iota((256, 256), 0) + iota((256, 256), 1) == 255)
    pick = ones_where((iota((40, 128), 1) == iota((40, 128), 0)) & (iota((40, 128), 0) < 33))
    for q in range(8):
        r, back = slice(q * 256, (q + 1) * 256), slice((7 - q) * 256, (8 - q) * 256)
        wcat[r, 0:128] = win_ref[r, :]
        shared = jnp.concatenate([wbc_ref[:, r].astype(F32), jnp.broadcast_to(wdt_ref[:, r].astype(F32), (8, 256))], axis=0)
        wcat[r, 128:256] = tn(shared.astype(BF), pick).astype(BF)
        wo[0:64, r] = wout_ref[:, r]
        wo[64:128, r] = nn(wout_ref[:, back], flip).astype(BF)
    for q in range(8):
        wf[q * 256:(q + 1) * 256, :] = nn(flip, wcat[(7 - q) * 256:(8 - q) * 256, :]).astype(BF)
    gap = jnp.zeros((1, 64), F32)
    taps = []
    for k in range(7):
        f_tap = conv_ref[k:k + 1, :] if k < 4 else gap
        r_tap = conv_ref[6 - k:7 - k, :] if k >= 3 else gap
        taps.append(jnp.concatenate([f_tap, r_tap], axis=1))

    for k in (-3, 3):
        z_arrival(k)
        for far in (3, 2, 1):
            carry(k, far if k < 0 else -far)
    for k in (-1, 1, -2, 2):
        z_arrival(k)
        spread(k)
    spread(-3)
    spread(3)
    x_arrivals(0)
    z_arrival(-6)
    carry(-6, 2)
    carry(-6, 1)
    z_arrival(6)
    carry(6, -1)
    for k in (-1, 1, -2, 2, -3, 3):
        x_arrivals(k)
    for k in (-4, 4, -5, 5):
        z_arrival(k)
        spread(k)
    spread(-6)
    spread(6)
    far_arrival(0)
    for k in (-7, 7, -8):
        z_arrival(k)
        spread(k)
    for k in (-4, 4, -5, 5, -6, 6):
        x_arrivals(k)
    for k in (-1, 1, -2, 2, -3, 3):
        far_arrival(k)
    for k in (-7, 7, -8):
        x_arrivals(k)
    for k in (-4, 4, -5, 5, -6, 6, -7, 7, -8):
        far_arrival(k)
    go(own.at[0, 63], hown.at[0], ys.at[0], yr.at[0], yp[0])
    go(own.at[0, 0], hown.at[1], ys.at[1], yr.at[1], yp[2])
    for n in range(64):
        arrived(oth.at[:, 0], cr.at[n])

    h_own, h_oth = own[0].reshape(ROWS, HALF), oth[0].reshape(ROWS, HALF)
    g_own, g_oth = own[1].reshape(ROWS, HALF), oth[1].reshape(ROWS, HALF)
    gg = nt(g_own, wo[:, mine]) + nt(g_oth, wo[:, theirs])
    gg_s[...] = gg
    pf = nn(h_own, wcat[mine, :]) + nn(h_oth, wcat[theirs, :])
    pr = nn(h_own, wf[mine, :]) + nn(h_oth, wf[theirs, :])
    lanes = fwd_lanes((ROWS, 128))
    x2 = jnp.where(lanes, pf[:, 0:128], pltpu.roll(pr[:, 0:128], 64, 1)).astype(BF).astype(F32)
    z2 = jnp.where(lanes, pltpu.roll(pf[:, 0:128], 64, 1), pr[:, 0:128]).astype(BF).astype(F32)
    x_scr[8:8 + ROWS, :] = x2
    z_s[...] = z2
    bf, br = pf[:, 128:256], pr[:, 128:256]
    bc_s[0] = bf.astype(BF)
    bc_s[1] = br.astype(BF)
    dtr = jnp.where(lanes, bf[:, 32:33], br[:, 32:33]) + bias
    dtr_s[...] = dtr
    dt = softplus(dtr)
    la = dt * rate
    dy = gg * (z2 * sigmoid(z2))
    for j in range(2):
        arrived(hown.at[j], yr.at[j])
        go(hown.at[j], hoth.at[j], hs_s.at[j], hs_r.at[j], other)
    low = ones_where(iota((CH, CH), 0) >= iota((CH, CH), 1))
    upp = ones_where(iota((CH, CH), 0) <= iota((CH, CH), 1))
    lanes, lane1, lane16 = fwd_lanes((CH, 128)), fwd_lanes((1, 128)), fwd_lanes((16, 128))
    ends, sts, ads, keeps = [], [], [], []
    for c in range(2):
        rows = slice(c * CH, (c + 1) * CH)
        cum = jnp.where(lanes, exact_left(low, la[rows]), exact_left(upp, la[rows]))
        cum_s[rows, :] = cum
        end = jnp.where(lane1, cum[CH - 1:CH], cum[0:1])
        ed = (jnp.exp(cum) * dy[rows]).astype(BF)
        b0, b1 = bf[rows].astype(BF), br[rows].astype(BF)
        ads.append(jnp.where(lane16, tn(b0, ed)[16:32], tn(b1, ed)[16:32]))
        ends.append(end)
        keeps.append((b0, b1, jnp.exp(end - cum)))
    for j in range(2):
        arrived(hoth.at[j], hs_r.at[j])
    e_own, e_oth = hown[...].reshape(16, HALF), hoth[...].reshape(16, HALF)
    xf = nn(e_own, wcat[mine, 0:128]) + nn(e_oth, wcat[theirs, 0:128])
    xb = nn(e_own, wf[mine, 0:128]) + nn(e_oth, wf[theirs, 0:128])
    edge = jnp.where(fwd_lanes((16, 128)), xf, pltpu.roll(xb, 64, 1)).astype(BF).astype(F32)
    x_scr[0:8, :] = jnp.where(y == 0, 0.0, edge[0:8])
    x_scr[8 + ROWS:EXT, :] = jnp.where(y == 3, 0.0, edge[8:16])
    pre = taps[0] * x_scr[5:5 + ROWS, :]
    for k in range(1, 7):
        pre = pre + taps[k] * x_scr[5 + k:5 + k + ROWS, :]
    pre_s[...] = pre
    u = dt * (pre * sigmoid(pre))

    for c in range(2):
        b0, b1, rem = keeps[c]
        ru = (rem * u[c * CH:(c + 1) * CH]).astype(BF)
        sts.append(jnp.where(lane16, tn(b0, ru)[0:16], tn(b1, ru)[0:16]))
    e0, e1 = jnp.exp(ends[0]), jnp.exp(ends[1])
    total_s[0:16, :] = jnp.where(lane16, e1 * sts[0] + sts[1], e0 * sts[1] + sts[0])
    total_s[16:32, :] = jnp.where(lane16, ads[0] + e0 * ads[1], ads[1] + e1 * ads[0])
    total_s[32:40, :] = jnp.broadcast_to(jnp.exp(ends[0] + ends[1]), (8, 128))
    all_s[y] = total_s[...]
    for k in range(3):
        go(total_s, all_s.at[y], st_s.at[k], st_r.at[k], yp[k])
    for k in range(3):
        arrived(all_s.at[lax.rem(y + 3 - k, 4)], st_r.at[k])
    nil = jnp.zeros((16, 128), F32)
    s_f, s_r, e_f, e_r = nil, nil, nil, nil
    for k in range(4):
        st, ad, dk = all_s[k, 0:16, :], all_s[k, 16:32, :], all_s[k, 32:33, :]
        s_f = jnp.where(k < y, dk * s_f + st, s_f)
        e_r = jnp.where(k < y, dk * e_r + ad, e_r)
    for k in (3, 2, 1, 0):
        st, ad, dk = all_s[k, 0:16, :], all_s[k, 16:32, :], all_s[k, 32:33, :]
        s_r = jnp.where(k > y, dk * s_r + st, s_r)
        e_f = jnp.where(k > y, dk * e_f + ad, e_f)
    state, adj = jnp.where(lane16, s_f, s_r), jnp.where(lane16, e_f, e_r)
    s_in = [jnp.where(lane16, state, e1 * state + sts[1]), jnp.where(lane16, e0 * state + sts[0], state)]
    e_out = [jnp.where(lane16, ads[1] + e1 * adj, adj), jnp.where(lane16, adj, ads[0] + e0 * adj)]
    s_out = [e0 * s_in[0] + sts[0], e1 * s_in[1] + sts[1]]

    same = ones_where((iota((128, 128), 0) < 64) == (iota((128, 128), 1) < 64))
    ii, jj = iota((CH, CH), 0), iota((CH, CH), 1)
    for c in range(2):
        rows = slice(c * CH, (c + 1) * CH)
        pre, zz, dtr, gg, cum = (r[rows, :] for r in (pre_s, z_s, dtr_s, gg_s, cum_s))
        sg, sz = sigmoid(pre), sigmoid(zz)
        xc, gate = pre * sg, zz * sz
        dt = softplus(dtr)
        u, dy = dt * xc, gg * gate
        ub, dyb = u.astype(BF), dy.astype(BF)
        rem, grow = jnp.exp(ends[c] - cum), jnp.exp(cum)
        cum_t = cum.T
        sb, eb = s_in[c].astype(BF), e_out[c].astype(BF)
        y_s, du_s, tails = [], [], []
        for s in range(2):
            bc = bc_s[s, rows, :]
            b, cc = bc[:, 0:16], bc[:, 16:32]
            col, across = cum[:, 64 * s:64 * s + 1], cum_t[64 * s:64 * s + 1, :]
            mask = (ii >= jj) if s == 0 else (ii <= jj)
            decay = jnp.exp(jnp.where(mask, col - across, -1e30))
            w = (nt(cc, b) * decay).astype(BF)
            rem_c, grow_c = rem[:, 64 * s:64 * s + 1], grow[:, 64 * s:64 * s + 1]
            y_s.append(nn(w, ub) + grow_c * nn(cc, sb))
            du_s.append(tn(w, dyb) + rem_c * nn(b, eb))
            half = lanes if s == 0 else jnp.logical_not(lanes)
            dym = jnp.where(half, dy, 0.0).astype(BF)
            um = jnp.where(half, u, 0.0).astype(BF)
            ds = (nt(dym, ub) * decay).astype(BF)
            dc = nn(ds, b) + grow_c * nt(dym, sb)
            db = tn(ds, cc) + rem_c * nt(um, eb)
            tails.append((db, dc))
        y2, du = jnp.where(lanes, y_s[0], y_s[1]), jnp.where(lanes, du_s[0], du_s[1])
        dl = exact_right(dyb.astype(F32) * y2 - ub.astype(F32) * du, same)
        direct = exact_right(du * xc, same)
        const = jnp.sum(e_out[c] * s_out[c], axis=0, keepdims=True)
        const = exact_right(jnp.broadcast_to(const, (16, 128)), same)[0:1]
        dla = jnp.where(lanes, exact_left(upp, dl), exact_left(low, dl)) + const
        ddt = (rate * dla + direct) * sigmoid(dtr)
        full = y2 + skip * xc
        gated_s[rows, :] = (full * gate).astype(BF)
        dz_s[rows, :] = gg * full * (sz * (1.0 + zz * (1.0 - sz)))
        dpre_s[rows, :] = (du * dt + skip * dy) * (sg * (1.0 + pre * (1.0 - sg)))
        for s in range(2):
            db, dc = tails[s]
            tail = jnp.concatenate([db, dc, ddt[:, 64 * s:64 * s + 1], jnp.zeros((CH, 95), F32)], axis=1).astype(BF)
            tail_s[rows, s * 128:(s + 1) * 128] = tail
            gcat[rows, s * 256 + 128:(s + 1) * 256] = tail

    go(dpre_s.at[ROWS - 8:ROWS, :], edge_s.at[0], ed_s.at[0], ed_r.at[0], yp[0])
    go(dpre_s.at[0:8, :], edge_s.at[1], ed_s.at[1], ed_r.at[1], yp[2])

    near, far = dev(x, y + 1 - 2 * lax.rem(y, 2), z, core), dev(x, 3 - y, z, core)
    turn, side = lax.rem((y + 1) // 2, 2), y // 2
    plan = ((near, turn, far, side), (far, side, near, turn))

    class Sum:
        def __init__(self, src, ref, size, b1, k1, b2, ss, rs):
            self.src, self.ref, self.size, self.b1, self.k1, self.b2, self.ss, self.rs = src, ref, size, b1, k1, b2, ss, rs

        def rows(self, k):
            return pl.ds(pl.multiple_of(k * self.size, self.size), self.size)

        def cols(self, h, k):
            return pl.ds(pl.multiple_of(h * 1024 + k * 512, 512), 512)

        def first(self):
            for h in range(2):
                p1, k1, _, _ = plan[h]
                go(self.src.at[self.rows(1 - k1), h * 1024:(h + 1) * 1024], self.b1.at[h], self.ss.at[h, 0], self.rs.at[h, 0], p1)

        def second(self):
            for h in range(2):
                _, k1, p2, k2 = plan[h]
                arrived(self.b1.at[h], self.rs.at[h, 0])
                for q in range(2):
                    c = slice(h * 1024 + q * 512, h * 1024 + (q + 1) * 512)
                    self.k1[h, q] = (self.src[self.rows(k1), c].astype(F32) + self.b1[h, :, q * 512:(q + 1) * 512].astype(F32)).astype(BF)
                go(self.k1.at[h, 1 - k2], self.b2.at[h], self.ss.at[h, 1], self.rs.at[h, 1], p2)

        def third(self):
            for h in range(2):
                _, k1, p2, k2 = plan[h]
                arrived(self.b2.at[h], self.rs.at[h, 1])
                at = (self.rows(k1), self.cols(h, k2))
                self.ref[at] = (self.k1[h, k2].astype(F32) + self.b2[h].astype(F32)).astype(BF)
                go(self.ref.at[at], self.ref.at[at], self.ss.at[h, 2], self.rs.at[h, 2], p2)

        def fourth(self):
            for h in range(2):
                p1, k1, _, k2 = plan[h]
                arrived(self.ref.at[self.rows(k1), self.cols(h, 1 - k2)], self.rs.at[h, 2])
                at = (self.rows(k1), slice(h * 1024, (h + 1) * 1024))
                go(self.ref.at[at], self.ref.at[at], self.ss.at[h, 3], self.rs.at[h, 3], p1)

        def last(self):
            for h in range(2):
                _, k1, _, _ = plan[h]
                arrived(self.ref.at[self.rows(1 - k1), h * 1024:(h + 1) * 1024], self.rs.at[h, 3])

    s_out_w = Sum(dwo, dwo_ref, 32, eo1, ko1, eo2, eo_s, eo_r)
    s_z = Sum(dwz, dwz_sum, 32, ez1, kz1, ez2, ez_s, ez_r)
    s_x = Sum(dwx, dwx_sum, 32, ei1, ki1, ei2, ei_s, ei_r)

    def both_strands(ref, lo):
        for q in range(8):
            c, back = slice(q * 256, (q + 1) * 256), slice((7 - q) * 256, (8 - q) * 256)
            ref[:, c] = ((acc[lo:lo + 64, c] + nn(acc[lo + 64:lo + 128, back].astype(BF), flip)) * SCALING).astype(BF)

    acc[0:128, mine] = tn(gated_s[...], own[1].reshape(ROWS, HALF))
    acc[0:128, theirs] = tn(gated_s[...], oth[1].reshape(ROWS, HALF))
    both_strands(dwo, 0)
    s_out_w.first()

    early = jnp.concatenate([tail_s[...], dz_s[...].astype(BF)], axis=1)
    acc[:, mine] = tn(early, own[0].reshape(ROWS, HALF))
    acc[:, theirs] = tn(early, oth[0].reshape(ROWS, HALF))
    for q in range(8):
        c, back = slice(q * 256, (q + 1) * 256), slice((7 - q) * 256, (8 - q) * 256)
        wb = ((acc[0:32, c] + nn(acc[128:160, back].astype(BF), flip)) * SCALING).astype(BF)
        m = (q % 4) * 2
        fb[q // 4, m * 32:(m + 1) * 32, :] = wb[:, 0:128]
        fb[q // 4, (m + 1) * 32:(m + 2) * 32, :] = wb[:, 128:256]
    go(fb.at[1 - core], fc, fc_s.at[0], fc_r.at[0], other)
    both_strands(dwz, 256)
    s_z.first()

    d_scr[8:8 + ROWS, :] = dpre_s[...]
    for j in range(2):
        arrived(edge_s.at[j], ed_r.at[j])
    d_scr[0:8, :] = jnp.where(y == 0, 0.0, edge_s[0])
    d_scr[8 + ROWS:EXT, :] = jnp.where(y == 3, 0.0, edge_s[1])
    dx = taps[6] * d_scr[5:5 + ROWS, :]
    for k in range(1, 7):
        dx = dx + taps[6 - k] * d_scr[5 + k:5 + k + ROWS, :]
    dz = dz_s[...]
    lanes = fwd_lanes((ROWS, 128))
    gcat[:, 0:128] = jnp.where(lanes, dx, pltpu.roll(dz, 64, 1)).astype(BF)
    gcat[:, 256:384] = jnp.where(lanes, pltpu.roll(dx, 64, 1), dz).astype(BF)

    arrived(fc, fc_r.at[0])
    for k in range(16):
        r = slice(k * 16, (k + 1) * 16)
        f1[k] = (fb[core, r, :].astype(F32) + fc[r, :].astype(F32)).astype(BF)
    for k in range(15):
        i, j = steps[k]
        go(f1.at[lax.rem(x + i, 4) * 4 + lax.rem(y + j, 4)], fx.at[k], fx_s.at[k], fx_r.at[k], plane[k])
    s_out_w.second()

    near_rows = pl.ds(pl.multiple_of(zh * 256, 256), 256)
    g_f, g_r = gcat[near_rows, 0:256], gcat[near_rows, 256:512]
    for who in range(2):
        for j in range(2):
            c = pl.ds(pl.multiple_of((core if who else 1 - core) * HALF + j * 512, 512), 512)
            gin[who, j] = (nt(g_f, wcat[c, :]) + nt(g_r, wf[c, :])).astype(BF)
            if who == 0:
                go(gin.at[0, j], rc.at[j], dc_s.at[j], dc_r.at[j], other)
    dxb = dx.astype(BF)
    acc[0:128, mine] = tn(dxb, own[0].reshape(ROWS, HALF))
    acc[0:128, theirs] = tn(dxb, oth[0].reshape(ROWS, HALF))
    both_strands(dwx, 0)
    s_x.first()
    part = f1[x * 4 + y].astype(F32)
    for k in range(15):
        arrived(fx.at[k], fx_r.at[k])
        part = part + fx[k].astype(F32)
    f2[...] = part.astype(BF)
    fz[zl] = part.astype(BF)
    for k in range(1, 8):
        go(f2, fz.at[zl], fz_s.at[k - 1], fz_r.at[k - 1], line(k))
    for j in range(2):
        arrived(rc.at[j], dc_r.at[j])
        for k in range(4):
            r = slice(k * 64, (k + 1) * 64)
            w1[j, k] = (gin[1, j, r, :].astype(F32) + rc[j, r, :].astype(F32)).astype(BF)
        for k in (2, 1, 3):
            go(w1.at[j, lax.rem(x + k, 4)], rx.at[j, k - 1], dx_s.at[j, k - 1], dx_r.at[j, k - 1], xp[k - 1])
    s_out_w.third()
    s_z.second()

    s_x.second()
    s_z.third()
    s_out_w.fourth()
    for k in range(1, 8):
        arrived(fz.at[lax.rem(zl + 8 - k, 8)], fz_r.at[k - 1])
    part = fz[0].astype(F32)
    for k in range(1, 8):
        part = part + fz[k].astype(F32)
    at = x * 4 + y
    fg[core, at] = part.astype(BF)
    for k in range(15):
        go(fg.at[core, at], fg.at[core, at], ga_s.at[k], ga_r.at[k], plane[k])
    s_x.third()
    s_z.fourth()
    for j in range(2):
        for k in (1, 3, 2):
            arrived(rx.at[j, k - 1], dx_r.at[j, k - 1])
        for k in range(8):
            r = slice(k * 8, (k + 1) * 8)
            w2[j, k] = (w1[j, x, r, :].astype(F32) + rx[j, 0, r, :].astype(F32) + rx[j, 1, r, :].astype(F32) + rx[j, 2, r, :].astype(F32)).astype(BF)
        for k in (4, 5, 3, 6, 2, 7, 1):
            go(w2.at[j, lax.rem(zl + k, 8)], rz.at[j, k - 1], dz_ss.at[j, k - 1], dz_rr.at[j, k - 1], line(k))
    s_x.fourth()
    for k in range(15):
        i, j = steps[k]
        arrived(fg.at[core, lax.rem(x + 4 - i, 4) * 4 + lax.rem(y + 4 - j, 4)], ga_r.at[k])
    go(fg.at[core], fg.at[core], fc_s.at[1], fc_r.at[1], other)
    for j in range(2):
        for k in range(1, 8):
            arrived(rz.at[j, k - 1], dz_rr.at[j, k - 1])
        hid = w2[j, zl].astype(F32)
        for k in range(7):
            hid = hid + rz[j, k].astype(F32)
        hs[:, j * 512:(j + 1) * 512] = hid.astype(BF)
    go(hs, hr, dc_s.at[2], dc_r.at[2], other)
    arrived(hr, dc_r.at[2])
    a, b = hs[...].astype(F32), hr[...].astype(F32)
    a, b = jnp.where(core == 0, a[0:4], a[4:8]), jnp.where(core == 0, b[0:4], b[4:8])
    hid_ref[:, 0:1024] = jnp.where(core == 0, a, b).astype(BF)
    hid_ref[:, 1024:2048] = jnp.where(core == 0, b, a).astype(BF)
    arrived(fg.at[1 - core], fc_r.at[1])
    for k in range(2):
        for m in range(16):
            c = slice(k * HALF + (m // 2) * 128, k * HALF + (m // 2 + 1) * 128)
            shared_ref[(m % 2) * 16:(m % 2 + 1) * 16, c] = fg[k, m]
    s_out_w.last()
    s_z.last()
    s_x.last()
    for q in range(16):
        r = slice(q * 128, (q + 1) * 128)
        turned = jnp.concatenate([dwx_sum[:, r].astype(F32), dwz_sum[:, r].astype(F32)], axis=0).T
        dwi_ref[r, :] = turned.astype(BF)
    for copy in pend:
        copy.wait_send()


def mixer(*args):
    def bf(*shape):
        return pltpu.VMEM(shape, BF)

    def f32(*shape):
        return pltpu.VMEM(shape, F32)

    def sems(*shape):
        return [pltpu.SemaphoreType.DMA(shape)] * 2

    def out(*shape):
        return jax.ShapeDtypeStruct(shape, BF)

    V, A = pl.BlockSpec(memory_space=pltpu.VMEM), pl.BlockSpec(memory_space=pl.ANY)
    scratch = [
        bf(4, D), bf(4, D), bf(D, 128), bf(32, D), bf(1, D), f32(4, 64), bf(64, D), pltpu.SemaphoreType.DMA((7,)),
        bf(2, 4, HALF), f32(8, HALF), bf(2, 64, 8, HALF), bf(2, 64, 8, HALF), bf(2, 8, HALF), bf(2, 8, HALF),
        bf(D, 256), bf(D, 256), bf(128, D), f32(EXT, 128), f32(EXT, 128),
        f32(ROWS, 128), f32(ROWS, 128), f32(ROWS, 128), f32(ROWS, 128), bf(2, ROWS, 128), f32(ROWS, 128),
        f32(40, 128), f32(4, 40, 128), bf(ROWS, 128), f32(ROWS, 128), f32(ROWS, 128), bf(ROWS, 256), f32(2, 8, 128),
        bf(ROWS, 512), f32(384, D), bf(64, D), bf(64, D), bf(64, D), bf(64, D), bf(64, D), bf(2, 16, 16, 128), bf(2, 2, 256, 512), bf(2, 256, 512), bf(2, 4, 64, 512), bf(2, 3, 64, 512), bf(2, 8, 8, 512), bf(2, 7, 8, 512),
        bf(8, HALF), bf(8, HALF),
        bf(2, 256, 128), bf(256, 128), bf(16, 16, 128), bf(15, 16, 128), bf(16, 128), bf(8, 16, 128),
        *[bf(2, 32, 1024), bf(2, 2, 32, 512), bf(2, 32, 512)] * 3,
        *sems(2), *sems(16), *sems(4, 16), *sems(64), *sems(2), *sems(2), *sems(3), *sems(2),
        *sems(3), *sems(2, 3), *sems(2, 7), *sems(2), *sems(15), *sems(7), *sems(15), *sems(2, 4), *sems(2, 4), *sems(2, 4),
    ]
    return pl.pallas_call(
        mixer_kernel,
        out_shape=(out(4, D), out(D, 128), out(64, D), out(32, D)),
        in_specs=[A] * 5 + [pl.BlockSpec(memory_space=pltpu.SMEM)] * 3 + [A] * 2, out_specs=[V] * 4, scratch_shapes=scratch,
        compiler_params=pltpu.CompilerParams(collective_id=0, has_side_effects=True, vmem_limit_bytes=56 << 20),
        name="mixer",
    )(*args)


def widen_kernel(*refs):
    sources, results, held, wide, sem_in, sem_out = refs[0:4], refs[4:8], refs[8:12], refs[12:16], refs[16], refs[17]
    ins = [pltpu.make_async_copy(sources[k], held[k], sem_in.at[k]) for k in range(4)]
    for copy in ins:
        copy.start()
    outs = []
    for k in (1, 2, 3, 0):
        ins[k].wait()
        wide[k][...] = held[k][...].astype(wide[k].dtype)
        outs.append(pltpu.make_async_copy(wide[k], results[k], sem_out.at[k]))
        outs[-1].start()
    for copy in outs:
        copy.wait()


def widen(*args):
    A = pl.BlockSpec(memory_space=pl.ANY)
    types = (BF, F32, F32, F32)
    return pl.pallas_call(
        widen_kernel,
        out_shape=tuple(jax.ShapeDtypeStruct(a.shape, t) for a, t in zip(args, types)),
        in_specs=[A] * 4, out_specs=[A] * 4,
        scratch_shapes=[pltpu.VMEM(a.shape, BF) for a in args] + [pltpu.VMEM(a.shape, t) for a, t in zip(args, types)]
        + [pltpu.SemaphoreType.DMA((4,))] * 2,
        compiler_params=pltpu.CompilerParams(vmem_limit_bytes=56 << 20),
        name="widen",
    )(*args)


def local(hidden, w_in, w_bc, w_dt, dt_bias, a_log, d_skip, conv_w, w_out, d_out):
    d_hidden, dwi, dwo, shared = mixer(hidden, d_out, w_in, w_bc.T, w_dt, dt_bias, a_log, d_skip, conv_w, w_out)
    d_hidden, d_w_in, d_w_out, d_w_bc = widen(d_hidden, dwi, dwo, shared)
    return (d_hidden, d_w_in, d_w_out, d_w_bc.T)


def solution(mesh):
    in_specs = (
        P(("ctx", "tp"), None), P(None, "tp"), P(), P("tp", None), P("tp"), P("tp"), P("tp"), P(None, "tp"),
        P("tp", None), P(("ctx", "tp"), None),
    )
    out_specs = (P(("ctx", "tp"), None), P(None, "tp"), P("tp", None), P())
    return jax.shard_map(local, mesh=mesh, in_specs=in_specs, out_specs=out_specs, check_vma=False)
```

```python
import math

import jax
import jax.numpy as jnp
from jax import lax
from jax.experimental import pallas as pl
from jax.experimental.pallas import tpu as pltpu
from jax.sharding import PartitionSpec as P

MESH = pl.DeviceIdType.MESH
BF, F32 = jnp.bfloat16, jnp.float32
ROWS, EXT, D, HALF, CH = 512, 528, 2048, 1024, 256
SCALING = 1.0 / math.sqrt(D)


def place():
    ctx, tp = lax.axis_index("ctx"), lax.axis_index("tp")
    y, zh = ctx // 2, ctx % 2
    x, zl, core = tp // 16, (tp // 2) % 8, tp % 2
    return x, y, zh * 8 + zl, core


def dev(x, y, z, core):
    return (y * 2 + z // 8, x * 16 + (z % 8) * 2 + core)


def greet(peers):
    barrier = pltpu.get_barrier_semaphore()
    for peer in peers:
        pl.semaphore_signal(barrier, inc=1, device_id=peer, device_id_type=MESH)
    pl.semaphore_wait(barrier, len(peers))


def remote(src, dst, ssem, rsem, peer):
    return pltpu.make_async_remote_copy(src_ref=src, dst_ref=dst, send_sem=ssem, recv_sem=rsem, device_id=peer, device_id_type=MESH)


def mm(a, b, dims):
    return lax.dot_general(a, b, (dims, ((), ())), preferred_element_type=F32)


def nn(a, b):
    return mm(a, b, ((1,), (0,)))


def nt(a, b):
    return mm(a, b, ((1,), (1,)))


def tn(a, b):
    return mm(a, b, ((0,), (0,)))


def iota(shape, dim):
    return lax.broadcasted_iota(jnp.int32, shape, dim)


def ones_where(mask):
    return mask.astype(F32).astype(BF)


def split3(v):
    h = v.astype(BF)
    m = (v - h.astype(F32)).astype(BF)
    l = (v - h.astype(F32) - m.astype(F32)).astype(BF)
    return h, m, l


def exact_left(t, v):
    h, m, l = split3(v)
    return (nn(t, l) + nn(t, m)) + nn(t, h)


def exact_right(v, t):
    h, m, l = split3(v)
    return (nn(l, t) + nn(m, t)) + nn(h, t)


def fwd_lanes(shape):
    return iota(shape, 1) < 64


def softplus(v):
    return jnp.maximum(v, 0.0) + jnp.log1p(jnp.exp(-jnp.abs(v)))


def sigmoid(v):
    return jax.nn.sigmoid(v)


def mixer_kernel(h_hbm, g_hbm, win_hbm, wbc_hbm, wdt_hbm, bias_ref, alog_ref, skip_ref, conv_hbm, wout_hbm,
                 hid_ref, dwi_ref, dwo_ref, shared_ref,
                 h_ref, g_ref, win_ref, wbc_ref, wdt_ref, conv_ref, wout_ref, in_sem, swap, asm, own, oth, hown, hoth, wcat, wf, wo, x_scr, d_scr,
                 pre_s, z_s, dtr_s, gg_s, bc_s, cum_s, total_s, all_s, gated_s, dpre_s, dz_s, tail_s, edge_s,
                 gcat, acc, dwx, dwx_sum, dwz, dwz_sum, dwo, fg, gin, rc, w1, rx, w2, rz, hs, hr,
                 fb, fc, f1, fx, f2, fz, ei1, ki1, ei2, ez1, kz1, ez2, eo1, ko1, eo2,
                 sw_s, sw_r, zs, zr, xs, xr, cs, cr, ys, yr, hs_s, hs_r, st_s, st_r, ed_s, ed_r,
                 dc_s, dc_r, dx_s, dx_r, dz_ss, dz_rr, fc_s, fc_r, fx_s, fx_r, fz_s, fz_r, ga_s, ga_r,
                 ei_s, ei_r, ez_s, ez_r, eo_s, eo_r):
    x, y, z, core = place()
    zh, zl = z // 8, z % 8
    bias, skip = bias_ref[0], skip_ref[0]
    rate = -jnp.exp(jnp.full((1, 128), alog_ref[0], F32))
    other = dev(x, y, z, 1 - core)
    xp = [dev(lax.rem(x + k, 4), y, z, core) for k in (1, 2, 3)]
    yp = [dev(x, lax.rem(y + k, 4), z, core) for k in (1, 2, 3)]
    steps = [(k // 4, k % 4) for k in range(1, 16)]
    plane = [dev(lax.rem(x + i, 4), lax.rem(y + j, 4), z, core) for i, j in steps]

    def along(k):
        return dev(x, y, lax.rem(z + 16 + k, 16), core)

    def line(k):
        return dev(x, y, zh * 8 + lax.rem(zl + k, 8), core)

    mine = pl.ds(pl.multiple_of(core * HALF, HALF), HALF)
    theirs = pl.ds(pl.multiple_of((1 - core) * HALF, HALF), HALF)
    pend = []

    def go(src, dst, ssem, rsem, peer):
        copy = remote(src, dst, ssem, rsem, peer)
        copy.start()
        pend.append(copy)
        return copy

    def arrived(dst, rsem):
        remote(dst, dst, sw_s.at[0], rsem, other).wait_recv()

    loads = []
    for src, dst in ((h_hbm, h_ref), (g_hbm, g_ref), (wdt_hbm, wdt_ref), (conv_hbm, conv_ref), (wbc_hbm, wbc_ref), (win_hbm, win_ref), (wout_hbm, wout_ref)):
        loads.append(pltpu.make_async_copy(src, dst, in_sem.at[len(loads)]))
        loads[-1].start()
    greet([other] + plane + [along(k) for k in (-3, -2, -1, 1, 2, 3)] + [line(k) for k in range(1, 8)])

    loads[0].wait()
    loads[1].wait()
    go(h_ref.at[:, theirs], swap.at[0], sw_s.at[0], sw_r.at[0], other)
    go(g_ref.at[:, theirs], swap.at[1], sw_s.at[1], sw_r.at[1], other)

    def blk(xx, k):
        zz = lax.rem(z + 16 + k, 16)
        return (zz // 8) * 32 + xx * 8 + zz % 8

    home = blk(x, 0)
    arrived(swap.at[0], sw_r.at[0])
    arrived(swap.at[1], sw_r.at[1])
    for k, ref in ((0, h_ref), (1, g_ref)):
        here, there = ref[:, mine].astype(F32), swap[k].astype(F32)
        asm[0:4, :] = jnp.where(core == 0, here, there)
        asm[4:8, :] = jnp.where(core == 0, there, here)
        own[k, home] = asm[...].astype(BF)

    def slot(k):
        return k if k >= 0 else 7 - k

    def cross(b, n):
        go(own.at[:, b], oth.at[:, b], cs.at[n], cr.at[n], other)

    def carry(k, far):
        b, n = blk(x, k), slot(k - far)
        go(own.at[:, b], own.at[:, b], zs.at[n], zr.at[n], along(far))

    def spread(k):
        b, n = blk(x, k), slot(k)
        go(own.at[:, b], own.at[:, b], xs.at[0, n], xr.at[0, n], xp[0])
        go(own.at[:, b], own.at[:, b], xs.at[1, n], xr.at[1, n], xp[2])
        cross(b, n)

    def z_arrival(k):
        arrived(own.at[:, blk(x, k)], zr.at[slot(k)])

    def x_arrivals(k):
        n = slot(k)
        b = blk(lax.rem(x + 3, 4), k)
        arrived(own.at[:, b], xr.at[0, n])
        go(own.at[0, b], own.at[0, b], xs.at[2, n], xr.at[2, n], xp[0])
        cross(b, 16 + n)
        b = blk(lax.rem(x + 1, 4), k)
        arrived(own.at[:, b], xr.at[1, n])
        go(own.at[1, b], own.at[1, b], xs.at[3, n], xr.at[3, n], xp[2])
        cross(b, 32 + n)

    def far_arrival(k):
        n, b = slot(k), blk(lax.rem(x + 2, 4), k)
        arrived(own.at[0, b], xr.at[2, n])
        arrived(own.at[1, b], xr.at[3, n])
        cross(b, 48 + n)

    for far in (3, -3, 2, -2, 1, -1):
        carry(0, far)
    spread(0)

    for copy in loads[2:]:
        copy.wait()
    flip = ones_where(iota((256, 256), 0) + iota((256, 256), 1) == 255)
    pick = ones_where((iota((40, 128), 1) == iota((40, 128), 0)) & (iota((40, 128), 0) < 33))
    for q in range(8):
        r, back = slice(q * 256, (q + 1) * 256), slice((7 - q) * 256, (8 - q) * 256)
        wcat[r, 0:128] = win_ref[r, :]
        shared = jnp.concatenate([wbc_ref[:, r].astype(F32), jnp.broadcast_to(wdt_ref[:, r].astype(F32), (8, 256))], axis=0)
        wcat[r, 128:256] = tn(shared.astype(BF), pick).astype(BF)
        wo[0:64, r] = wout_ref[:, r]
        wo[64:128, r] = nn(wout_ref[:, back], flip).astype(BF)
    for q in range(8):
        wf[q * 256:(q + 1) * 256, :] = nn(flip, wcat[(7 - q) * 256:(8 - q) * 256, :]).astype(BF)
    gap = jnp.zeros((1, 64), F32)
    taps = []
    for k in range(7):
        f_tap = conv_ref[k:k + 1, :] if k < 4 else gap
        r_tap = conv_ref[6 - k:7 - k, :] if k >= 3 else gap
        taps.append(jnp.concatenate([f_tap, r_tap], axis=1))

    for k in (-3, 3):
        z_arrival(k)
        for far in (3, 2, 1):
            carry(k, far if k < 0 else -far)
    for k in (-1, 1, -2, 2):
        z_arrival(k)
        spread(k)
    spread(-3)
    spread(3)
    x_arrivals(0)
    z_arrival(-6)
    carry(-6, 2)
    carry(-6, 1)
    z_arrival(6)
    carry(6, -1)
    for k in (-1, 1, -2, 2, -3, 3):
        x_arrivals(k)
    for k in (-4, 4, -5, 5):
        z_arrival(k)
        spread(k)
    spread(-6)
    spread(6)
    far_arrival(0)
    for k in (-7, 7, -8):
        z_arrival(k)
        spread(k)
    for k in (-4, 4, -5, 5, -6, 6):
        x_arrivals(k)
    for k in (-1, 1, -2, 2, -3, 3):
        far_arrival(k)
    for k in (-7, 7, -8):
        x_arrivals(k)
    for k in (-4, 4, -5, 5, -6, 6, -7, 7, -8):
        far_arrival(k)
    go(own.at[0, 63], hown.at[0], ys.at[0], yr.at[0], yp[0])
    go(own.at[0, 0], hown.at[1], ys.at[1], yr.at[1], yp[2])
    for n in range(64):
        arrived(oth.at[:, 0], cr.at[n])

    h_own, h_oth = own[0].reshape(ROWS, HALF), oth[0].reshape(ROWS, HALF)
    g_own, g_oth = own[1].reshape(ROWS, HALF), oth[1].reshape(ROWS, HALF)
    gg = nt(g_own, wo[:, mine]) + nt(g_oth, wo[:, theirs])
    gg_s[...] = gg
    pf = nn(h_own, wcat[mine, :]) + nn(h_oth, wcat[theirs, :])
    pr = nn(h_own, wf[mine, :]) + nn(h_oth, wf[theirs, :])
    lanes = fwd_lanes((ROWS, 128))
    x2 = jnp.where(lanes, pf[:, 0:128], pltpu.roll(pr[:, 0:128], 64, 1)).astype(BF).astype(F32)
    z2 = jnp.where(lanes, pltpu.roll(pf[:, 0:128], 64, 1), pr[:, 0:128]).astype(BF).astype(F32)
    x_scr[8:8 + ROWS, :] = x2
    z_s[...] = z2
    bf, br = pf[:, 128:256], pr[:, 128:256]
    bc_s[0] = bf.astype(BF)
    bc_s[1] = br.astype(BF)
    dtr = jnp.where(lanes, bf[:, 32:33], br[:, 32:33]) + bias
    dtr_s[...] = dtr
    dt = softplus(dtr)
    la = dt * rate
    dy = gg * (z2 * sigmoid(z2))
    for j in range(2):
        arrived(hown.at[j], yr.at[j])
        go(hown.at[j], hoth.at[j], hs_s.at[j], hs_r.at[j], other)
    low = ones_where(iota((CH, CH), 0) >= iota((CH, CH), 1))
    upp = ones_where(iota((CH, CH), 0) <= iota((CH, CH), 1))
    lanes, lane1, lane16 = fwd_lanes((CH, 128)), fwd_lanes((1, 128)), fwd_lanes((16, 128))
    ends, sts, ads, keeps = [], [], [], []
    for c in range(2):
        rows = slice(c * CH, (c + 1) * CH)
        cum = jnp.where(lanes, exact_left(low, la[rows]), exact_left(upp, la[rows]))
        cum_s[rows, :] = cum
        end = jnp.where(lane1, cum[CH - 1:CH], cum[0:1])
        ed = (jnp.exp(cum) * dy[rows]).astype(BF)
        b0, b1 = bf[rows].astype(BF), br[rows].astype(BF)
        ads.append(jnp.where(lane16, tn(b0, ed)[16:32], tn(b1, ed)[16:32]))
        ends.append(end)
        keeps.append((b0, b1, jnp.exp(end - cum)))
    for j in range(2):
        arrived(hoth.at[j], hs_r.at[j])
    e_own, e_oth = hown[...].reshape(16, HALF), hoth[...].reshape(16, HALF)
    xf = nn(e_own, wcat[mine, 0:128]) + nn(e_oth, wcat[theirs, 0:128])
    xb = nn(e_own, wf[mine, 0:128]) + nn(e_oth, wf[theirs, 0:128])
    edge = jnp.where(fwd_lanes((16, 128)), xf, pltpu.roll(xb, 64, 1)).astype(BF).astype(F32)
    x_scr[0:8, :] = jnp.where(y == 0, 0.0, edge[0:8])
    x_scr[8 + ROWS:EXT, :] = jnp.where(y == 3, 0.0, edge[8:16])
    pre = taps[0] * x_scr[5:5 + ROWS, :]
    for k in range(1, 7):
        pre = pre + taps[k] * x_scr[5 + k:5 + k + ROWS, :]
    pre_s[...] = pre
    u = dt * (pre * sigmoid(pre))

    for c in range(2):
        b0, b1, rem = keeps[c]
        ru = (rem * u[c * CH:(c + 1) * CH]).astype(BF)
        sts.append(jnp.where(lane16, tn(b0, ru)[0:16], tn(b1, ru)[0:16]))
    e0, e1 = jnp.exp(ends[0]), jnp.exp(ends[1])
    total_s[0:16, :] = jnp.where(lane16, e1 * sts[0] + sts[1], e0 * sts[1] + sts[0])
    total_s[16:32, :] = jnp.where(lane16, ads[0] + e0 * ads[1], ads[1] + e1 * ads[0])
    total_s[32:40, :] = jnp.broadcast_to(jnp.exp(ends[0] + ends[1]), (8, 128))
    all_s[y] = total_s[...]
    for k in range(3):
        go(total_s, all_s.at[y], st_s.at[k], st_r.at[k], yp[k])
    for k in range(3):
        arrived(all_s.at[lax.rem(y + 3 - k, 4)], st_r.at[k])
    nil = jnp.zeros((16, 128), F32)
    s_f, s_r, e_f, e_r = nil, nil, nil, nil
    for k in range(4):
        st, ad, dk = all_s[k, 0:16, :], all_s[k, 16:32, :], all_s[k, 32:33, :]
        s_f = jnp.where(k < y, dk * s_f + st, s_f)
        e_r = jnp.where(k < y, dk * e_r + ad, e_r)
    for k in (3, 2, 1, 0):
        st, ad, dk = all_s[k, 0:16, :], all_s[k, 16:32, :], all_s[k, 32:33, :]
        s_r = jnp.where(k > y, dk * s_r + st, s_r)
        e_f = jnp.where(k > y, dk * e_f + ad, e_f)
    state, adj = jnp.where(lane16, s_f, s_r), jnp.where(lane16, e_f, e_r)
    s_in = [jnp.where(lane16, state, e1 * state + sts[1]), jnp.where(lane16, e0 * state + sts[0], state)]
    e_out = [jnp.where(lane16, ads[1] + e1 * adj, adj), jnp.where(lane16, adj, ads[0] + e0 * adj)]
    s_out = [e0 * s_in[0] + sts[0], e1 * s_in[1] + sts[1]]

    same = ones_where((iota((128, 128), 0) < 64) == (iota((128, 128), 1) < 64))
    ii, jj = iota((CH, CH), 0), iota((CH, CH), 1)
    for c in range(2):
        rows = slice(c * CH, (c + 1) * CH)
        pre, zz, dtr, gg, cum = (r[rows, :] for r in (pre_s, z_s, dtr_s, gg_s, cum_s))
        sg, sz = sigmoid(pre), sigmoid(zz)
        xc, gate = pre * sg, zz * sz
        dt = softplus(dtr)
        u, dy = dt * xc, gg * gate
        ub, dyb = u.astype(BF), dy.astype(BF)
        rem, grow = jnp.exp(ends[c] - cum), jnp.exp(cum)
        cum_t = cum.T
        sb, eb = s_in[c].astype(BF), e_out[c].astype(BF)
        y_s, du_s, tails = [], [], []
        for s in range(2):
            bc = bc_s[s, rows, :]
            b, cc = bc[:, 0:16], bc[:, 16:32]
            col, across = cum[:, 64 * s:64 * s + 1], cum_t[64 * s:64 * s + 1, :]
            mask = (ii >= jj) if s == 0 else (ii <= jj)
            decay = jnp.exp(jnp.where(mask, col - across, -1e30))
            w = (nt(cc, b) * decay).astype(BF)
            rem_c, grow_c = rem[:, 64 * s:64 * s + 1], grow[:, 64 * s:64 * s + 1]
            y_s.append(nn(w, ub) + grow_c * nn(cc, sb))
            du_s.append(tn(w, dyb) + rem_c * nn(b, eb))
            half = lanes if s == 0 else jnp.logical_not(lanes)
            dym = jnp.where(half, dy, 0.0).astype(BF)
            um = jnp.where(half, u, 0.0).astype(BF)
            ds = (nt(dym, ub) * decay).astype(BF)
            dc = nn(ds, b) + grow_c * nt(dym, sb)
            db = tn(ds, cc) + rem_c * nt(um, eb)
            tails.append((db, dc))
        y2, du = jnp.where(lanes, y_s[0], y_s[1]), jnp.where(lanes, du_s[0], du_s[1])
        dl = exact_right(dyb.astype(F32) * y2 - ub.astype(F32) * du, same)
        direct = exact_right(du * xc, same)
        const = jnp.sum(e_out[c] * s_out[c], axis=0, keepdims=True)
        const = exact_right(jnp.broadcast_to(const, (16, 128)), same)[0:1]
        dla = jnp.where(lanes, exact_left(upp, dl), exact_left(low, dl)) + const
        ddt = (rate * dla + direct) * sigmoid(dtr)
        full = y2 + skip * xc
        gated_s[rows, :] = (full * gate).astype(BF)
        dz_s[rows, :] = gg * full * (sz * (1.0 + zz * (1.0 - sz)))
        dpre_s[rows, :] = (du * dt + skip * dy) * (sg * (1.0 + pre * (1.0 - sg)))
        for s in range(2):
            db, dc = tails[s]
            tail = jnp.concatenate([db, dc, ddt[:, 64 * s:64 * s + 1], jnp.zeros((CH, 95), F32)], axis=1).astype(BF)
            tail_s[rows, s * 128:(s + 1) * 128] = tail
            gcat[rows, s * 256 + 128:(s + 1) * 256] = tail

    go(dpre_s.at[ROWS - 8:ROWS, :], edge_s.at[0], ed_s.at[0], ed_r.at[0], yp[0])
    go(dpre_s.at[0:8, :], edge_s.at[1], ed_s.at[1], ed_r.at[1], yp[2])

    near, far = dev(x, y + 1 - 2 * lax.rem(y, 2), z, core), dev(x, 3 - y, z, core)
    turn, side = lax.rem((y + 1) // 2, 2), y // 2
    plan = ((near, turn, far, side), (far, side, near, turn))

    class Sum:
        def __init__(self, src, ref, size, b1, k1, b2, ss, rs):
            self.src, self.ref, self.size, self.b1, self.k1, self.b2, self.ss, self.rs = src, ref, size, b1, k1, b2, ss, rs

        def rows(self, k):
            return pl.ds(pl.multiple_of(k * self.size, self.size), self.size)

        def cols(self, h, k):
            return pl.ds(pl.multiple_of(h * 1024 + k * 512, 512), 512)

        def first(self):
            for h in range(2):
                p1, k1, _, _ = plan[h]
                go(self.src.at[self.rows(1 - k1), h * 1024:(h + 1) * 1024], self.b1.at[h], self.ss.at[h, 0], self.rs.at[h, 0], p1)

        def second(self):
            for h in range(2):
                _, k1, p2, k2 = plan[h]
                arrived(self.b1.at[h], self.rs.at[h, 0])
                for q in range(2):
                    c = slice(h * 1024 + q * 512, h * 1024 + (q + 1) * 512)
                    self.k1[h, q] = (self.src[self.rows(k1), c].astype(F32) + self.b1[h, :, q * 512:(q + 1) * 512].astype(F32)).astype(BF)
                go(self.k1.at[h, 1 - k2], self.b2.at[h], self.ss.at[h, 1], self.rs.at[h, 1], p2)

        def third(self):
            for h in range(2):
                _, k1, p2, k2 = plan[h]
                arrived(self.b2.at[h], self.rs.at[h, 1])
                at = (self.rows(k1), self.cols(h, k2))
                self.ref[at] = (self.k1[h, k2].astype(F32) + self.b2[h].astype(F32)).astype(BF)
                go(self.ref.at[at], self.ref.at[at], self.ss.at[h, 2], self.rs.at[h, 2], p2)

        def fourth(self):
            for h in range(2):
                p1, k1, _, k2 = plan[h]
                arrived(self.ref.at[self.rows(k1), self.cols(h, 1 - k2)], self.rs.at[h, 2])
                at = (self.rows(k1), slice(h * 1024, (h + 1) * 1024))
                go(self.ref.at[at], self.ref.at[at], self.ss.at[h, 3], self.rs.at[h, 3], p1)

        def last(self):
            for h in range(2):
                _, k1, _, _ = plan[h]
                arrived(self.ref.at[self.rows(1 - k1), h * 1024:(h + 1) * 1024], self.rs.at[h, 3])

    s_out_w = Sum(dwo, dwo_ref, 32, eo1, ko1, eo2, eo_s, eo_r)
    s_z = Sum(dwz, dwz_sum, 32, ez1, kz1, ez2, ez_s, ez_r)
    s_x = Sum(dwx, dwx_sum, 32, ei1, ki1, ei2, ei_s, ei_r)

    def both_strands(ref, lo):
        for q in range(8):
            c, back = slice(q * 256, (q + 1) * 256), slice((7 - q) * 256, (8 - q) * 256)
            ref[:, c] = ((acc[lo:lo + 64, c] + nn(acc[lo + 64:lo + 128, back].astype(BF), flip)) * SCALING).astype(BF)

    acc[0:128, mine] = tn(gated_s[...], own[1].reshape(ROWS, HALF))
    acc[0:128, theirs] = tn(gated_s[...], oth[1].reshape(ROWS, HALF))
    both_strands(dwo, 0)
    s_out_w.first()

    early = jnp.concatenate([tail_s[...], dz_s[...].astype(BF)], axis=1)
    acc[:, mine] = tn(early, own[0].reshape(ROWS, HALF))
    acc[:, theirs] = tn(early, oth[0].reshape(ROWS, HALF))
    for q in range(8):
        c, back = slice(q * 256, (q + 1) * 256), slice((7 - q) * 256, (8 - q) * 256)
        wb = ((acc[0:32, c] + nn(acc[128:160, back].astype(BF), flip)) * SCALING).astype(BF)
        m = (q % 4) * 2
        fb[q // 4, m * 32:(m + 1) * 32, :] = wb[:, 0:128]
        fb[q // 4, (m + 1) * 32:(m + 2) * 32, :] = wb[:, 128:256]
    go(fb.at[1 - core], fc, fc_s.at[0], fc_r.at[0], other)
    both_strands(dwz, 256)
    s_z.first()

    d_scr[8:8 + ROWS, :] = dpre_s[...]
    for j in range(2):
        arrived(edge_s.at[j], ed_r.at[j])
    d_scr[0:8, :] = jnp.where(y == 0, 0.0, edge_s[0])
    d_scr[8 + ROWS:EXT, :] = jnp.where(y == 3, 0.0, edge_s[1])
    dx = taps[6] * d_scr[5:5 + ROWS, :]
    for k in range(1, 7):
        dx = dx + taps[6 - k] * d_scr[5 + k:5 + k + ROWS, :]
    dz = dz_s[...]
    lanes = fwd_lanes((ROWS, 128))
    gcat[:, 0:128] = jnp.where(lanes, dx, pltpu.roll(dz, 64, 1)).astype(BF)
    gcat[:, 256:384] = jnp.where(lanes, pltpu.roll(dx, 64, 1), dz).astype(BF)

    arrived(fc, fc_r.at[0])
    for k in range(16):
        r = slice(k * 16, (k + 1) * 16)
        f1[k] = (fb[core, r, :].astype(F32) + fc[r, :].astype(F32)).astype(BF)
    for k in range(15):
        i, j = steps[k]
        go(f1.at[lax.rem(x + i, 4) * 4 + lax.rem(y + j, 4)], fx.at[k], fx_s.at[k], fx_r.at[k], plane[k])
    s_out_w.second()

    near_rows = pl.ds(pl.multiple_of(zh * 256, 256), 256)
    g_f, g_r = gcat[near_rows, 0:256], gcat[near_rows, 256:512]
    for who in range(2):
        for j in range(4):
            c = pl.ds(pl.multiple_of((core if who else 1 - core) * HALF + j * 256, 256), 256)
            gin[who, j] = (nt(g_f, wcat[c, :]) + nt(g_r, wf[c, :])).astype(BF)
            if who == 0:
                go(gin.at[0, j], rc.at[j], dc_s.at[j], dc_r.at[j], other)
    dxb = dx.astype(BF)
    acc[0:128, mine] = tn(dxb, own[0].reshape(ROWS, HALF))
    acc[0:128, theirs] = tn(dxb, oth[0].reshape(ROWS, HALF))
    both_strands(dwx, 0)
    s_x.first()
    part = f1[x * 4 + y].astype(F32)
    for k in range(15):
        arrived(fx.at[k], fx_r.at[k])
        part = part + fx[k].astype(F32)
    f2[...] = part.astype(BF)
    fz[zl] = part.astype(BF)
    for k in range(1, 8):
        go(f2, fz.at[zl], fz_s.at[k - 1], fz_r.at[k - 1], line(k))
    for j in range(4):
        arrived(rc.at[j], dc_r.at[j])
        for k in range(4):
            r = slice(k * 64, (k + 1) * 64)
            w1[j, k] = (gin[1, j, r, :].astype(F32) + rc[j, r, :].astype(F32)).astype(BF)
        for k in (2, 1, 3):
            go(w1.at[j, lax.rem(x + k, 4)], rx.at[j, k - 1], dx_s.at[j, k - 1], dx_r.at[j, k - 1], xp[k - 1])
    s_out_w.third()
    s_z.second()

    s_x.second()
    s_z.third()
    s_out_w.fourth()
    for k in range(1, 8):
        arrived(fz.at[lax.rem(zl + 8 - k, 8)], fz_r.at[k - 1])
    part = fz[0].astype(F32)
    for k in range(1, 8):
        part = part + fz[k].astype(F32)
    at = x * 4 + y
    fg[core, at] = part.astype(BF)
    for k in range(15):
        go(fg.at[core, at], fg.at[core, at], ga_s.at[k], ga_r.at[k], plane[k])
    s_x.third()
    s_z.fourth()
    for j in range(4):
        for k in (1, 3, 2):
            arrived(rx.at[j, k - 1], dx_r.at[j, k - 1])
        for k in range(8):
            r = slice(k * 8, (k + 1) * 8)
            w2[j, k] = (w1[j, x, r, :].astype(F32) + rx[j, 0, r, :].astype(F32) + rx[j, 1, r, :].astype(F32) + rx[j, 2, r, :].astype(F32)).astype(BF)
        for k in (4, 5, 3, 6, 2, 7, 1):
            go(w2.at[j, lax.rem(zl + k, 8)], rz.at[j, k - 1], dz_ss.at[j, k - 1], dz_rr.at[j, k - 1], line(k))
    s_x.fourth()
    for k in range(15):
        i, j = steps[k]
        arrived(fg.at[core, lax.rem(x + 4 - i, 4) * 4 + lax.rem(y + 4 - j, 4)], ga_r.at[k])
    go(fg.at[core], fg.at[core], fc_s.at[1], fc_r.at[1], other)
    for j in range(4):
        for k in range(1, 8):
            arrived(rz.at[j, k - 1], dz_rr.at[j, k - 1])
        hid = w2[j, zl].astype(F32)
        for k in range(7):
            hid = hid + rz[j, k].astype(F32)
        hs[:, j * 256:(j + 1) * 256] = hid.astype(BF)
    go(hs, hr, dc_s.at[4], dc_r.at[4], other)
    arrived(hr, dc_r.at[4])
    a, b = hs[...].astype(F32), hr[...].astype(F32)
    a, b = jnp.where(core == 0, a[0:4], a[4:8]), jnp.where(core == 0, b[0:4], b[4:8])
    hid_ref[:, 0:1024] = jnp.where(core == 0, a, b).astype(BF)
    hid_ref[:, 1024:2048] = jnp.where(core == 0, b, a).astype(BF)
    arrived(fg.at[1 - core], fc_r.at[1])
    for k in range(2):
        for m in range(16):
            c = slice(k * HALF + (m // 2) * 128, k * HALF + (m // 2 + 1) * 128)
            shared_ref[(m % 2) * 16:(m % 2 + 1) * 16, c] = fg[k, m]
    s_out_w.last()
    s_z.last()
    s_x.last()
    for q in range(16):
        r = slice(q * 128, (q + 1) * 128)
        turned = jnp.concatenate([dwx_sum[:, r].astype(F32), dwz_sum[:, r].astype(F32)], axis=0).T
        dwi_ref[r, :] = turned.astype(BF)
    for copy in pend:
        copy.wait_send()


def mixer(*args):
    def bf(*shape):
        return pltpu.VMEM(shape, BF)

    def f32(*shape):
        return pltpu.VMEM(shape, F32)

    def sems(*shape):
        return [pltpu.SemaphoreType.DMA(shape)] * 2

    def out(*shape):
        return jax.ShapeDtypeStruct(shape, BF)

    V, A = pl.BlockSpec(memory_space=pltpu.VMEM), pl.BlockSpec(memory_space=pl.ANY)
    scratch = [
        bf(4, D), bf(4, D), bf(D, 128), bf(32, D), bf(1, D), f32(4, 64), bf(64, D), pltpu.SemaphoreType.DMA((7,)),
        bf(2, 4, HALF), f32(8, HALF), bf(2, 64, 8, HALF), bf(2, 64, 8, HALF), bf(2, 8, HALF), bf(2, 8, HALF),
        bf(D, 256), bf(D, 256), bf(128, D), f32(EXT, 128), f32(EXT, 128),
        f32(ROWS, 128), f32(ROWS, 128), f32(ROWS, 128), f32(ROWS, 128), bf(2, ROWS, 128), f32(ROWS, 128),
        f32(40, 128), f32(4, 40, 128), bf(ROWS, 128), f32(ROWS, 128), f32(ROWS, 128), bf(ROWS, 256), f32(2, 8, 128),
        bf(ROWS, 512), f32(384, D), bf(64, D), bf(64, D), bf(64, D), bf(64, D), bf(64, D), bf(2, 16, 16, 128), bf(2, 4, 256, 256), bf(4, 256, 256), bf(4, 4, 64, 256), bf(4, 3, 64, 256), bf(4, 8, 8, 256), bf(4, 7, 8, 256),
        bf(8, HALF), bf(8, HALF),
        bf(2, 256, 128), bf(256, 128), bf(16, 16, 128), bf(15, 16, 128), bf(16, 128), bf(8, 16, 128),
        *[bf(2, 32, 1024), bf(2, 2, 32, 512), bf(2, 32, 512)] * 3,
        *sems(2), *sems(16), *sems(4, 16), *sems(64), *sems(2), *sems(2), *sems(3), *sems(2),
        *sems(5), *sems(4, 3), *sems(4, 7), *sems(2), *sems(15), *sems(7), *sems(15), *sems(2, 4), *sems(2, 4), *sems(2, 4),
    ]
    return pl.pallas_call(
        mixer_kernel,
        out_shape=(out(4, D), out(D, 128), out(64, D), out(32, D)),
        in_specs=[A] * 5 + [pl.BlockSpec(memory_space=pltpu.SMEM)] * 3 + [A] * 2, out_specs=[V] * 4, scratch_shapes=scratch,
        compiler_params=pltpu.CompilerParams(collective_id=0, has_side_effects=True, vmem_limit_bytes=56 << 20),
        name="mixer",
    )(*args)


def widen_kernel(*refs):
    sources, results, held, wide, sem_in, sem_out = refs[0:4], refs[4:8], refs[8:12], refs[12:16], refs[16], refs[17]
    ins = [pltpu.make_async_copy(sources[k], held[k], sem_in.at[k]) for k in range(4)]
    for copy in ins:
        copy.start()
    outs = []
    for k in (1, 2, 3, 0):
        ins[k].wait()
        wide[k][...] = held[k][...].astype(wide[k].dtype)
        outs.append(pltpu.make_async_copy(wide[k], results[k], sem_out.at[k]))
        outs[-1].start()
    for copy in outs:
        copy.wait()


def widen(*args):
    A = pl.BlockSpec(memory_space=pl.ANY)
    types = (BF, F32, F32, F32)
    return pl.pallas_call(
        widen_kernel,
        out_shape=tuple(jax.ShapeDtypeStruct(a.shape, t) for a, t in zip(args, types)),
        in_specs=[A] * 4, out_specs=[A] * 4,
        scratch_shapes=[pltpu.VMEM(a.shape, BF) for a in args] + [pltpu.VMEM(a.shape, t) for a, t in zip(args, types)]
        + [pltpu.SemaphoreType.DMA((4,))] * 2,
        compiler_params=pltpu.CompilerParams(vmem_limit_bytes=56 << 20),
        name="widen",
    )(*args)


def local(hidden, w_in, w_bc, w_dt, dt_bias, a_log, d_skip, conv_w, w_out, d_out):
    d_hidden, dwi, dwo, shared = mixer(hidden, d_out, w_in, w_bc.T, w_dt, dt_bias, a_log, d_skip, conv_w, w_out)
    d_hidden, d_w_in, d_w_out, d_w_bc = widen(d_hidden, dwi, dwo, shared)
    return (d_hidden, d_w_in, d_w_out, d_w_bc.T)


def solution(mesh):
    in_specs = (
        P(("ctx", "tp"), None), P(None, "tp"), P(), P("tp", None), P("tp"), P("tp"), P("tp"), P(None, "tp"),
        P("tp", None), P(("ctx", "tp"), None),
    )
    out_specs = (P(("ctx", "tp"), None), P(None, "tp"), P("tp", None), P())
    return jax.shard_map(local, mesh=mesh, in_specs=in_specs, out_specs=out_specs, check_vma=False)
```
